32 devices in a mesh: dp: 4 (over y, x), ctx: 8 (over z, core).
Axes of the slice: x: 2, y: 2, z: 4, core: 2. Of those that a mesh axis runs over, the one named last changes fastest.
Arguments:
- query_rows: bfloat16 [4, 1024, 1024], P('dp', 'ctx'), may hold values from -0.59765625 to 0.59765625
- key_rows: bfloat16 [4, 1024, 1024], P('dp', 'ctx'), may hold values from -0.59765625 to 0.59765625
- value_rows: bfloat16 [4, 1024, 2048], P('dp', 'ctx'), may hold values from -6 to 6
- log_decay: bfloat16 [4, 1024, 1024], P('dp', 'ctx'), may hold values from -1 to 0, as said below
- out_grad: bfloat16 [4, 1024, 2048], P('dp', 'ctx'), may hold values from -1.796875 to 1.796875
- doc_ids: int32 [4, 1024], P('dp', 'ctx'), may hold values from 0 to 3, as said below
- block_order: int32 [4, 8, 4], P(None, 'ctx'), may hold values from 0 to 3, each once within a row
Outputs:
- attn_out: bfloat16 [4, 1024, 2048], P('dp', 'ctx')
- query_grad: bfloat16 [4, 1024, 1024], P('dp', 'ctx')
- key_grad: bfloat16 [4, 1024, 1024], P('dp', 'ctx')
- value_grad: bfloat16 [4, 1024, 2048], P('dp', 'ctx')
- decay_grad: bfloat16 [4, 1024, 1024], P('dp', 'ctx')
The draws below stay inside these ranges and needn't reach their ends.
Inputs may be any that keep to these rules, and one draw needn't show every extreme that they name: `log_decay`: nonpositive. `doc_ids`: never falls along a pack; every document number of a pack is used; each document has 1 to 512 positions, one of them exactly 512 and one 8 or fewer. `block_order`: each row of a device's list names each of its 4 blocks once.
All inputs are finite; a program needn't handle non-finite values.
Results may differ from the reference program's by a relative error of at most 0.0015.
Values may be sent and summed in bfloat16 or wider, within the bound.
A program may use at most 192 MiB of HBM per device.

```python
import jax
import jax.numpy as jnp
from jax import lax

HEADS = 16
DK = 64
DV = 128
TOK_DEV = 128
BLK = 32
DOCS = 4
PACKED_SEQUENCES = 4
PACK_POSITIONS = 1024
HK = 1024
HV = 2048
NB = 4
N_CTX = 8


def draw_log_decay(key, part):
    every_key = jax.random.split(key, 7)
    fast_share = 0.5
    fast_pick = jax.random.uniform(every_key[0], (HK,)) < fast_share
    fast_rate = jnp.exp(jax.random.uniform(every_key[1], (HK,), minval=jnp.log(0.02), maxval=jnp.log(0.05)))
    slow_rate = jnp.exp(jax.random.uniform(every_key[2], (HK,), minval=jnp.log(0.05 / PACK_POSITIONS), maxval=jnp.log(0.3 / PACK_POSITIONS)))
    every_rate = jnp.where(fast_pick, fast_rate, slow_rate)
    pieces_n = PACK_POSITIONS // TOK_DEV
    split_multiplier = jnp.exp(jax.random.uniform(every_key[3], (PACKED_SEQUENCES, pieces_n, 1, HK), minval=jnp.log(0.5), maxval=jnp.log(2.0)))
    split_multiplier = jnp.broadcast_to(split_multiplier, (PACKED_SEQUENCES, pieces_n, TOK_DEV, HK)).reshape(PACKED_SEQUENCES, PACK_POSITIONS, HK)
    random_offset = jax.random.uniform(every_key[4], (PACKED_SEQUENCES, PACK_POSITIONS, HK), minval=0.5, maxval=1.5)
    spike_position = (jax.random.uniform(every_key[5], (PACKED_SEQUENCES, PACK_POSITIONS, 1)) < 2.0 / PACK_POSITIONS).astype(jnp.float32)
    spike_length = jax.random.uniform(every_key[6], (PACKED_SEQUENCES, PACK_POSITIONS, 1), minval=0.2, maxval=0.5)
    gate_values = -(every_rate[None, None, :] * split_multiplier * random_offset) - spike_position * spike_length
    return gate_values.astype(jnp.float32).astype(jnp.bfloat16)


def draw_one_pack(pack_key):
    every_key = jax.random.split(pack_key, 3)
    half_len = PACK_POSITIONS // 2
    short_len = jax.random.randint(every_key[0], (), 1, 9).astype(jnp.int32)
    rest_len = (PACK_POSITIONS - half_len - short_len).astype(jnp.int32)
    third_len = jax.random.randint(every_key[1], (), 1, rest_len).astype(jnp.int32)
    lengths = jnp.stack([jnp.int32(half_len), short_len, third_len, rest_len - third_len]).astype(jnp.int32)
    order_pick = jax.random.permutation(every_key[2], DOCS)
    lengths = lengths[order_pick]
    ends = jnp.cumsum(lengths)[:DOCS - 1].astype(jnp.int32)
    positions = jnp.arange(PACK_POSITIONS, dtype=jnp.int32)
    return jnp.sum((positions[:, None] >= ends[None, :]).astype(jnp.int32), axis=1).astype(jnp.int32)


def draw_doc_ids(key, part):
    pack_keys = jax.random.split(jax.random.fold_in(key, 17), PACKED_SEQUENCES)
    return jax.vmap(draw_one_pack)(pack_keys).astype(jnp.int32)


def levels(own_key, dims, pieces, least, top_value):
    gain = 1.0
    for position, blocks in pieces:
        draws = jax.random.uniform(jax.random.fold_in(jax.random.fold_in(own_key, 6), position), (blocks,), jnp.float32, least / len(pieces), top_value / len(pieces))
        gain = gain * jnp.repeat(jnp.exp(draws), dims[position] // blocks).reshape((-1,) + (1,) * (len(dims) - 1 - position))
    return gain


def gaussian(own_key, shape, width, limit, cuts=(), kind=jnp.bfloat16):
    values = width * jax.random.normal(own_key, shape, jnp.float32)
    if cuts:
        values = values * levels(own_key, shape, cuts, -0.22, 0.18)
    return jnp.clip(values, -limit, limit).astype(kind)


def setup_inputs(seed: int = 0) -> dict:
    streams_of = jax.random.split(jax.random.key(seed), 8)
    query_rows = gaussian(streams_of[0], (PACKED_SEQUENCES, PACK_POSITIONS, HK), 0.1, 0.59765625, ((0, 4), (1, 8)))
    key_rows = gaussian(streams_of[1], (PACKED_SEQUENCES, PACK_POSITIONS, HK), 0.1, 0.59765625, ((0, 4), (1, 8)))
    value_rows = gaussian(streams_of[2], (PACKED_SEQUENCES, PACK_POSITIONS, HV), 1.0, 6.0, ((0, 4), (1, 8)))
    log_decay = draw_log_decay(jax.random.fold_in(streams_of[7], 71), 0)
    out_grad = gaussian(streams_of[4], (PACKED_SEQUENCES, PACK_POSITIONS, HV), 0.3, 1.796875, ((0, 4), (1, 8)))
    doc_ids = draw_doc_ids(jax.random.fold_in(streams_of[7], 71), 0)
    block_order = jax.vmap(lambda own: jax.random.permutation(own, NB))(jax.random.split(streams_of[6], PACKED_SEQUENCES * N_CTX)).reshape((PACKED_SEQUENCES, N_CTX, NB)).astype(jnp.int32)
    return {"query_rows": query_rows, "key_rows": key_rows, "value_rows": value_rows, "log_decay": log_decay, "out_grad": out_grad, "doc_ids": doc_ids, "block_order": block_order}


HIGH = lax.Precision.HIGHEST

def prepare(query_b, key_b, value_b, decay_b, doc_row):
    row_count = query_b.shape[0]
    head_count = query_b.shape[1] // DK
    query_f = query_b.astype(jnp.float32).reshape(row_count, head_count, DK)
    key_f = key_b.astype(jnp.float32).reshape(row_count, head_count, DK)
    value_f = value_b.astype(jnp.float32).reshape(row_count, head_count, DV)
    cumul = jnp.cumsum(decay_b.astype(jnp.float32).reshape(row_count, head_count, DK), axis=0)
    total_log = cumul[-1]
    growth = jnp.exp(cumul)
    shrink = jnp.exp(-cumul)
    to_end = jnp.exp(total_log[None] - cumul)
    later_pos = lax.broadcasted_iota(jnp.int32, (row_count, row_count), 0)
    earlier_pos = lax.broadcasted_iota(jnp.int32, (row_count, row_count), 1)
    same_doc = ((later_pos >= earlier_pos) & (doc_row[:, None] == doc_row[None, :])).astype(jnp.float32)
    first_id = doc_row[0]
    last_id = doc_row[-1]
    in_first = (doc_row == first_id).astype(jnp.float32)[:, None, None]
    in_last = (doc_row == last_id).astype(jnp.float32)[:, None, None]
    query_t = query_f * growth
    key_t = key_f * shrink
    scores = jnp.einsum('thi,shi->hts', query_t, key_t, precision=HIGH) * same_doc[None]
    return {'query_f': query_f, 'key_f': key_f, 'value_f': value_f, 'growth': growth, 'shrink': shrink, 'to_end': to_end, 'same_doc': same_doc, 'first_id': first_id, 'last_id': last_id, 'in_first': in_first, 'in_last': in_last, 'query_t': query_t, 'key_t': key_t, 'scores': scores, 'decay_all': jnp.exp(total_log)}

def state_end(parts):
    return jnp.einsum('shi,shj->hij', parts['key_f'] * parts['to_end'] * parts['in_last'], parts['value_f'], precision=HIGH)

def start_grad(parts, grad_f):
    factor = DK ** (-0.5)
    return factor * jnp.einsum('thi,thj->hij', parts['query_t'] * parts['in_first'], grad_f, precision=HIGH)

def finish(parts, grad_f, state_in, use_state, carry_in, use_carry):
    factor = DK ** (-0.5)
    head_w = parts['in_first'] * use_state
    tail_w = parts['in_last'] * use_carry
    attn_rows = factor * (jnp.einsum('hts,shj->thj', parts['scores'], parts['value_f'], precision=HIGH) + jnp.einsum('thi,hij->thj', parts['query_t'], state_in, precision=HIGH) * head_w)
    grad_scores = jnp.einsum('thj,shj->hts', grad_f, parts['value_f'], precision=HIGH) * parts['same_doc'][None]
    grad_query = factor * parts['growth'] * (jnp.einsum('hts,shi->thi', grad_scores, parts['key_t'], precision=HIGH) + jnp.einsum('thj,hij->thi', grad_f, state_in, precision=HIGH) * head_w)
    grad_value = factor * jnp.einsum('hts,thj->shj', parts['scores'], grad_f, precision=HIGH) + jnp.einsum('shi,hij->shj', parts['key_f'] * parts['to_end'], carry_in, precision=HIGH) * tail_w
    grad_key = factor * parts['shrink'] * jnp.einsum('hts,thi->shi', grad_scores, parts['query_t'], precision=HIGH) + parts['to_end'] * jnp.einsum('hij,shj->shi', carry_in, parts['value_f'], precision=HIGH) * tail_w
    grad_log = parts['query_f'] * grad_query - parts['key_f'] * grad_key
    sum_start = lax.optimization_barrier(jnp.sum(grad_log * parts['in_first'], axis=0))
    return (attn_rows, grad_query, grad_key, grad_value, grad_log, sum_start)

def decay_grad_of(parts, grad_log, sums_in, use_carry):
    inside = jnp.einsum('ts,thi->shi', parts['same_doc'], grad_log, precision=HIGH)
    return inside + sums_in[None] * parts['in_last'] * use_carry

def move_in(raw_array, inverse):
    packs_n, seq_len, chans = raw_array.shape
    pieces_n = inverse.shape[1]
    block_n = inverse.shape[2]
    per_peer = block_n // packs_n
    blocks_all = raw_array.reshape(packs_n, pieces_n, block_n, BLK, chans)
    index_all = jnp.broadcast_to(inverse[:, :, :, None, None], blocks_all.shape)
    sent = jnp.take_along_axis(blocks_all, index_all, axis=2)
    sent = sent.reshape(packs_n, pieces_n, packs_n, per_peer, BLK, chans)
    return jnp.transpose(sent, (2, 1, 0, 3, 4, 5)).reshape(packs_n, seq_len, chans)

def move_out(balanced, order_all):
    packs_n, seq_len, chans = balanced.shape
    pieces_n = order_all.shape[1]
    block_n = order_all.shape[2]
    per_peer = block_n // packs_n
    parted = balanced.reshape(packs_n, pieces_n, packs_n, per_peer, BLK, chans)
    parted = jnp.transpose(parted, (2, 1, 0, 3, 4, 5)).reshape(packs_n, pieces_n, block_n, BLK, chans)
    index_all = jnp.broadcast_to(order_all[:, :, :, None, None], parted.shape)
    return jnp.take_along_axis(parted, index_all, axis=2).reshape(packs_n, seq_len, chans)

def one_pack(pack_in):
    query_p, key_p, value_p, decay_p, grad_p, doc_p = pack_in
    pieces_n = PACK_POSITIONS // TOK_DEV
    query_c = query_p.reshape(pieces_n, TOK_DEV, HK)
    key_c = key_p.reshape(pieces_n, TOK_DEV, HK)
    value_c = value_p.reshape(pieces_n, TOK_DEV, HV)
    decay_c = decay_p.reshape(pieces_n, TOK_DEV, HK)
    grad_c = grad_p.reshape(pieces_n, TOK_DEV, HV)
    doc_c = doc_p.reshape(pieces_n, TOK_DEV)

    def forward_step(carried, piece_in):
        state_in, prior_last = carried
        parts = prepare(*piece_in)
        use_state = (prior_last == parts['first_id']).astype(jnp.float32)
        single = (parts['first_id'] == parts['last_id']).astype(jnp.float32)
        state_out = state_end(parts) + single * use_state * parts['decay_all'][..., None] * state_in
        return ((state_out, parts['last_id']), (state_in, use_state))
    start = (jnp.zeros((HEADS, DK, DV), jnp.float32), jnp.int32(-1))
    unused_end, (states_in, uses_in) = lax.scan(forward_step, start, (query_c, key_c, value_c, decay_c, doc_c))

    def reverse_step(carried, piece_in):
        carry_in, sums_in, next_first = carried
        query_b, key_b, value_b, decay_b, doc_row, grad_b, state_in, use_state = piece_in
        parts = prepare(query_b, key_b, value_b, decay_b, doc_row)
        grad_f = grad_b.astype(jnp.float32).reshape(TOK_DEV, HEADS, DV)
        use_carry = (next_first == parts['last_id']).astype(jnp.float32)
        single = (parts['first_id'] == parts['last_id']).astype(jnp.float32)
        attn_rows, grad_query, grad_key, grad_value, grad_log, sum_start = finish(parts, grad_f, state_in, use_state, carry_in, use_carry)
        grad_decay = decay_grad_of(parts, grad_log, sums_in, use_carry)
        carry_out = start_grad(parts, grad_f) + single * use_carry * parts['decay_all'][..., None] * carry_in
        sums_out = sum_start + single * use_carry * sums_in
        results = (attn_rows.reshape(TOK_DEV, HV), grad_query.reshape(TOK_DEV, HK), grad_key.reshape(TOK_DEV, HK), grad_value.reshape(TOK_DEV, HV), grad_decay.reshape(TOK_DEV, HK))
        return ((carry_out, sums_out, parts['first_id']), results)
    start_back = (jnp.zeros((HEADS, DK, DV), jnp.float32), jnp.zeros((HEADS, DK), jnp.float32), jnp.int32(-1))
    unused_back, results = lax.scan(reverse_step, start_back, (query_c, key_c, value_c, decay_c, doc_c, grad_c, states_in, uses_in), reverse=True)
    return tuple((item.reshape(PACK_POSITIONS, item.shape[-1]) for item in results))

def reference(query_rows, key_rows, value_rows, log_decay, out_grad, doc_ids, block_order):
    inverse = jnp.argsort(block_order, axis=2).astype(jnp.int32)
    query_bal = move_in(query_rows, inverse)
    key_bal = move_in(key_rows, inverse)
    value_bal = move_in(value_rows, inverse)
    decay_bal = move_in(log_decay, inverse)
    attn_all, query_all, key_all, value_all, decay_all = lax.map(one_pack, (query_bal, key_bal, value_bal, decay_bal, out_grad, doc_ids))
    attn_out = attn_all.astype(jnp.bfloat16)
    query_grad = move_out(query_all.astype(jnp.bfloat16), block_order)
    key_grad = move_out(key_all.astype(jnp.bfloat16), block_order)
    value_grad = move_out(value_all.astype(jnp.bfloat16), block_order)
    decay_grad = move_out(decay_all.astype(jnp.bfloat16), block_order)
    return (attn_out, query_grad, key_grad, value_grad, decay_grad)
```

```python
import functools

import jax
import jax.numpy as jnp
from jax import lax
from jax.experimental import pallas as pl
from jax.experimental.pallas import tpu as pltpu
from jax.sharding import PartitionSpec as P

DK = 64
DV = 128
BLK = 32
KW = 2 * DK
VW = 2 * DV
W = 3 * KW + VW
MESH = pl.DeviceIdType.MESH
F32 = jnp.float32
BF16 = jnp.bfloat16

NN = (((1,), (0,)), ((), ()))
NT = (((1,), (1,)), ((), ()))
TN = (((0,), (0,)), ((), ()))


def split(x):
    hi = x.astype(BF16)
    return hi, (x - hi.astype(F32)).astype(BF16)


def dot(a, b, dims):
    a = a if isinstance(a, tuple) else (a,)
    b = b if isinstance(b, tuple) else (b,)
    total = None
    for i, left in enumerate(a):
        for j, right in enumerate(b):
            if i + j > 1:
                continue
            term = lax.dot_general(left, right, dims, preferred_element_type=F32)
            total = term if total is None else total + term
    return total


def both(fn, pair):
    return tuple(fn(x) for x in pair)


def kernel(
    n_dp, n_ctx, order_ref, doc_ref, q_ref, k_ref, v_ref, d_ref, g_ref,
    out_ref, dq_ref, dk_ref, dv_ref, dd_ref,
    sx, rx, sy, ry, f_own, f_in, b_own, b_in, doc_prev, doc_next,
    x_send, x_recv, y_send, y_recv, f_send, f_recv, b_send, b_recv, doc_send, doc_recv,
):
    me = lax.axis_index("dp")
    pos = lax.axis_index("ctx")
    rows = q_ref.shape[1]
    pairs = q_ref.shape[2] // KW
    blocks = rows // BLK
    per = blocks // n_dp
    part = per * BLK
    has_prev = pos > 0
    has_next = pos < n_ctx - 1

    barrier = pltpu.get_barrier_semaphore()
    for r in range(1, n_dp):
        peer = lax.rem(me + r, n_dp)
        pl.semaphore_signal(barrier, inc=1, device_id={"dp": peer}, device_id_type=MESH)

    @pl.when(has_prev)
    def _():
        pl.semaphore_signal(barrier, inc=1, device_id={"ctx": pos - 1}, device_id_type=MESH)

    @pl.when(has_next)
    def _():
        pl.semaphore_signal(barrier, inc=1, device_id={"ctx": pos + 1}, device_id_type=MESH)

    def my_rows(index):
        return pl.ds(pl.multiple_of(index * part, part), part)

    def lanes(h, width):
        return pl.ds(pl.multiple_of(h * width, width), width)

    order = [order_ref[me, 0, j] for j in range(blocks)]

    def piece(j):
        return slice(j * BLK, (j + 1) * BLK)

    def stage(h, carry):
        for src, width, at in ((q_ref, KW, 0), (k_ref, KW, KW), (d_ref, KW, 2 * KW), (v_ref, VW, 3 * KW)):
            parts = [src[0, piece(j), lanes(h, width)] for j in range(blocks)]
            for dest in range(blocks):
                chosen = parts[0]
                for j in range(1, blocks):
                    chosen = lax.select(order[j] == dest, parts[j], chosen)
                sx[h, piece(dest), at : at + width] = chosen
        rx[h, my_rows(me), :] = sx[h, my_rows(me), :]
        return carry

    lax.fori_loop(0, pairs, stage, 0)

    @pl.when(jnp.logical_not(has_prev))
    def _():
        doc_prev[...] = jnp.full_like(doc_prev, -1)
        f_in[...] = jnp.zeros_like(f_in)

    @pl.when(jnp.logical_not(has_next))
    def _():
        doc_next[...] = jnp.full_like(doc_next, -1)
        b_in[...] = jnp.zeros_like(b_in)

    peers = n_dp - 1 + has_prev.astype(jnp.int32) + has_next.astype(jnp.int32)
    pl.semaphore_wait(barrier, peers)

    def exchange(src, dst, send, recv, h, r):
        peer = lax.rem(me + r, n_dp)
        return pltpu.make_async_remote_copy(
            src_ref=src.at[h, my_rows(peer), :],
            dst_ref=dst.at[h, my_rows(me), :],
            send_sem=send.at[h, r],
            recv_sem=recv.at[h, r],
            device_id={"dp": peer},
            device_id_type=MESH,
        )

    def arrival(src, dst, send, recv, h, r):
        source = lax.rem(me + n_dp - r, n_dp)
        return pltpu.make_async_remote_copy(
            src_ref=src.at[h, my_rows(source), :],
            dst_ref=dst.at[h, my_rows(source), :],
            send_sem=send.at[h, r],
            recv_sem=recv.at[h, r],
            device_id={"dp": source},
            device_id_type=MESH,
        )

    def neighbour(src, dst, send, recv, step):
        return pltpu.make_async_remote_copy(
            src_ref=src, dst_ref=dst, send_sem=send, recv_sem=recv,
            device_id={"ctx": pos + step}, device_id_type=MESH,
        )

    def doc_up():
        return neighbour(doc_ref, doc_prev, doc_send.at[0], doc_recv.at[0], 1)

    def doc_down():
        return neighbour(doc_ref, doc_next, doc_send.at[1], doc_recv.at[1], -1)

    def chain_up(h):
        return neighbour(f_own.at[h], f_in.at[h], f_send.at[h], f_recv.at[h], 1)

    def chain_down(h):
        return neighbour(b_own.at[h], b_in.at[h], b_send.at[h], b_recv.at[h], -1)

    @pl.when(has_next)
    def _():
        doc_up().start()

    @pl.when(has_prev)
    def _():
        doc_down().start()

    def send_rows(h, carry):
        for r in range(1, n_dp):
            exchange(sx, rx, x_send, x_recv, h, r).start()
        return carry

    lax.fori_loop(0, pairs, send_rows, 0)

    @pl.when(has_prev)
    def _():
        doc_up().wait_recv()

    @pl.when(has_next)
    def _():
        doc_down().wait_recv()

    doc_row = jnp.broadcast_to(doc_ref[...].astype(F32), (rows, rows))
    doc_col = doc_row.T
    first_row = doc_col[0:1, :]
    last_row = doc_col[rows - 1 : rows, :]
    prev_last = jnp.broadcast_to(doc_prev[:, rows - 1 : rows].astype(F32), (1, rows))
    next_first = jnp.broadcast_to(doc_next[:, 0:1].astype(F32), (1, rows))
    use_state = (prev_last == first_row).astype(F32)
    use_carry = (next_first == last_row).astype(F32)
    single = (first_row == last_row).astype(F32)
    pass_state = single * use_state
    pass_carry = single * use_carry
    in_first = (doc_col == first_row).astype(F32)
    in_last = (doc_col == last_row).astype(F32)
    head_w = in_first * use_state
    tail_w = in_last * use_carry
    row_id = lax.broadcasted_iota(jnp.int32, (rows, rows), 0)
    lane_id = lax.broadcasted_iota(jnp.int32, (rows, rows), 1)
    same = (doc_row == doc_col) & (row_id >= lane_id)
    later = ((doc_row == doc_col) & (row_id <= lane_id)).astype(BF16)
    lower = (row_id >= lane_id).astype(BF16)
    in_a = lax.broadcasted_iota(jnp.int32, (rows, KW), 1) < DK
    factor = DK ** (-0.5)

    def load(h):
        q = rx[h, :, 0:KW]
        k = rx[h, :, KW : 2 * KW]
        d = rx[h, :, 2 * KW : 3 * KW]
        v = rx[h, :, 3 * KW : W]
        g = g_ref[0, :, lanes(h, VW)]
        cum = dot(lower, d, NN)
        total = cum[rows - 1 : rows, :]
        growth = jnp.exp(cum)
        shrink = jnp.exp(-cum)
        to_end = jnp.exp(total - cum)
        q_f = q.astype(F32)
        k_f = k.astype(F32)
        return q_f, k_f, v, g, d, growth, shrink, to_end

    def fold(wide):
        return jnp.concatenate([wide[0:DK, 0:DV], wide[DK:KW, DV:VW]], axis=0)

    def spread(tall):
        nil = jnp.zeros((DK, DV), tall.dtype)
        top = jnp.concatenate([tall[0:DK], nil], axis=1)
        low = jnp.concatenate([nil, tall[DK:KW]], axis=1)
        return jnp.concatenate([top, low], axis=0)

    def local(h, carry):
        for r in range(1, n_dp):
            arrival(sx, rx, x_send, x_recv, h, r).wait_recv()
        q_f, k_f, v, g, d, growth, shrink, to_end = load(h)
        f_own[h] = fold(dot(split(k_f * to_end * in_last), v, TN))
        b_own[h] = factor * fold(dot(split(q_f * growth * in_first), g, TN))
        return carry

    lax.fori_loop(0, pairs, local, 0)

    def decay_of(h):
        d = rx[h, :, 2 * KW : 3 * KW]
        return jnp.exp(dot(d, jnp.ones((rows, DV), BF16), TN))

    def finish(h):
        q_f, k_f, v, g, d, growth, shrink, to_end = load(h)
        q_t = q_f * growth
        k_t = k_f * shrink
        k_e = k_f * to_end * tail_w
        zero = jnp.zeros_like(q_t)
        q_2 = split(jnp.concatenate([jnp.where(in_a, q_t, zero), jnp.where(in_a, zero, q_t)], axis=0))
        k_s = split(k_t)
        k_2 = split(jnp.concatenate([jnp.where(in_a, k_t, zero), jnp.where(in_a, zero, k_t)], axis=0))
        same_2 = jnp.concatenate([same, same], axis=0)
        score_2 = split(jnp.where(same_2, dot(q_2, k_s, NT), 0.0))
        v_a, v_b = v[:, 0:DV], v[:, DV:VW]
        g_a, g_b = g[:, 0:DV], g[:, DV:VW]
        score_a = both(lambda x: x[0:rows], score_2)
        score_b = both(lambda x: x[rows : 2 * rows], score_2)
        state = both(spread, split(f_in[h]))
        carry = both(spread, split(b_in[h]))
        near = jnp.concatenate([dot(score_a, v_a, NN), dot(score_b, v_b, NN)], axis=1)
        far = dot(split(q_t * head_w), state, NN)
        out_ref[0, :, lanes(h, VW)] = (factor * (near + far)).astype(BF16)
        gs_a = jnp.where(same, dot(g_a, v_a, NT), 0.0)
        gs_b = jnp.where(same, dot(g_b, v_b, NT), 0.0)
        dq_near = dot(split(jnp.concatenate([gs_a, gs_b], axis=1)), k_2, NN)
        dq = factor * growth * (dq_near + dot(g, state, NT) * head_w)
        dk_near = dot(split(jnp.concatenate([gs_a, gs_b], axis=0)), q_2, TN)
        dk = factor * shrink * dk_near + to_end * dot(v, carry, NT) * tail_w
        dv_near = jnp.concatenate([dot(score_a, g_a, TN), dot(score_b, g_b, TN)], axis=1)
        dv = factor * dv_near + dot(split(k_e), carry, NN)
        log_grad = q_f * dq - k_f * dk
        sums = dot(jnp.ones((8, DV), BF16), split(f_own[h] * b_in[h]), NT)
        dd = dot(later, split(log_grad), NN) + sums[0:1] * tail_w
        sy[h, :, 0:KW] = dq.astype(BF16)
        sy[h, :, KW : 2 * KW] = dk.astype(BF16)
        sy[h, :, 2 * KW : 3 * KW] = dd.astype(BF16)
        sy[h, :, 3 * KW : W] = dv.astype(BF16)
        ry[h, my_rows(me), :] = sy[h, my_rows(me), :]
        for r in range(1, n_dp):
            exchange(sy, ry, y_send, y_recv, h, r).start()

    below = n_ctx - 1 - pos
    last_of = jnp.maximum(pos, below)

    def step(t, carry):
        up = t - pos
        down = t - below
        ready = t - last_of

        @pl.when((up >= 0) & (up < pairs))
        def _():
            @pl.when(has_prev)
            def _():
                chain_up(up).wait_recv()

            f_own[up] = f_own[up] + pass_state * decay_of(up) * f_in[up]

            @pl.when(has_next)
            def _():
                chain_up(up).start()

        @pl.when((down >= 0) & (down < pairs))
        def _():
            @pl.when(has_next)
            def _():
                chain_down(down).wait_recv()

            b_own[down] = b_own[down] + pass_carry * decay_of(down) * b_in[down]

            @pl.when(has_prev)
            def _():
                chain_down(down).start()

        @pl.when((ready >= 0) & (ready < pairs))
        def _():
            finish(ready)

        return carry

    lax.fori_loop(0, n_ctx - 1 + pairs, step, 0)

    def wait_back(h, carry):
        for r in range(1, n_dp):
            arrival(sy, ry, y_send, y_recv, h, r).wait_recv()
        return carry

    lax.fori_loop(0, pairs, wait_back, 0)

    def unpack(h, carry):
        for dst, width, at in ((dq_ref, KW, 0), (dk_ref, KW, KW), (dd_ref, KW, 2 * KW), (dv_ref, VW, 3 * KW)):
            parts = [ry[h, piece(j), at : at + width] for j in range(blocks)]
            for j in range(blocks):
                chosen = parts[0]
                for place in range(1, blocks):
                    chosen = lax.select(order[j] == place, parts[place], chosen)
                dst[0, piece(j), lanes(h, width)] = chosen
        return carry

    lax.fori_loop(0, pairs, unpack, 0)

    def drain(h, carry):
        for r in range(1, n_dp):
            exchange(sx, rx, x_send, x_recv, h, r).wait_send()
            exchange(sy, ry, y_send, y_recv, h, r).wait_send()

        @pl.when(has_next)
        def _():
            chain_up(h).wait_send()

        @pl.when(has_prev)
        def _():
            chain_down(h).wait_send()

        return carry

    lax.fori_loop(0, pairs, drain, 0)

    @pl.when(has_next)
    def _():
        doc_up().wait_send()

    @pl.when(has_prev)
    def _():
        doc_down().wait_send()


def body(n_dp, n_ctx, query_rows, key_rows, value_rows, log_decay, out_grad, doc_ids, block_order):
    rows, hk = query_rows.shape[1:]
    hv = value_rows.shape[2]
    pairs = hk // KW
    vmem = pl.BlockSpec(memory_space=pltpu.VMEM)
    keys = jax.ShapeDtypeStruct((1, rows, hk), BF16)
    values = jax.ShapeDtypeStruct((1, rows, hv), BF16)
    dma = pltpu.SemaphoreType.DMA
    out, dq, dk, dv, dd = pl.pallas_call(
        functools.partial(kernel, n_dp, n_ctx),
        out_shape=(values, keys, keys, values, keys),
        in_specs=[pl.BlockSpec(memory_space=pltpu.SMEM)] + [vmem] * 6,
        out_specs=(vmem,) * 5,
        scratch_shapes=[
            pltpu.VMEM((pairs, rows, W), BF16),
            pltpu.VMEM((pairs, rows, W), BF16),
            pltpu.VMEM((pairs, rows, W), BF16),
            pltpu.VMEM((pairs, rows, W), BF16),
            pltpu.VMEM((pairs, KW, DV), F32),
            pltpu.VMEM((pairs, KW, DV), F32),
            pltpu.VMEM((pairs, KW, DV), F32),
            pltpu.VMEM((pairs, KW, DV), F32),
            pltpu.VMEM((1, rows), jnp.int32),
            pltpu.VMEM((1, rows), jnp.int32),
            dma((pairs, n_dp)), dma((pairs, n_dp)), dma((pairs, n_dp)), dma((pairs, n_dp)),
            dma((pairs,)), dma((pairs,)), dma((pairs,)), dma((pairs,)),
            dma((2,)), dma((2,)),
        ],
        compiler_params=pltpu.CompilerParams(
            collective_id=0, has_side_effects=True, vmem_limit_bytes=40 * 1024 * 1024
        ),
    )(block_order, doc_ids, query_rows, key_rows, value_rows, log_decay, out_grad)
    return out, dq, dk, dv, dd


def solution(mesh):
    placed = P("dp", "ctx", None)
    return jax.shard_map(
        functools.partial(body, mesh.shape["dp"], mesh.shape["ctx"]),
        mesh=mesh,
        in_specs=(placed,) * 5 + (P("dp", "ctx"), P(None, "ctx", None)),
        out_specs=(placed,) * 5,
        check_vma=False,
    )
```

```python
import functools

import jax
import jax.numpy as jnp
from jax import lax
from jax.experimental import pallas as pl
from jax.experimental.pallas import tpu as pltpu
from jax.sharding import PartitionSpec as P

DK = 64
DV = 128
BLK = 32
KW = 2 * DK
VW = 2 * DV
W = 3 * KW + VW
MESH = pl.DeviceIdType.MESH
F32 = jnp.float32
BF16 = jnp.bfloat16

NN = (((1,), (0,)), ((), ()))
NT = (((1,), (1,)), ((), ()))
TN = (((0,), (0,)), ((), ()))


def split(x):
    hi = x.astype(BF16)
    return hi, (x - hi.astype(F32)).astype(BF16)


def dot(a, b, dims):
    a = a if isinstance(a, tuple) else (a,)
    b = b if isinstance(b, tuple) else (b,)
    total = None
    for i, left in enumerate(a):
        for j, right in enumerate(b):
            if i + j > 1:
                continue
            term = lax.dot_general(left, right, dims, preferred_element_type=F32)
            total = term if total is None else total + term
    return total


def both(fn, pair):
    return tuple(fn(x) for x in pair)


def kernel(
    n_dp, n_ctx, order_hbm, doc_hbm, q_hbm, k_hbm, v_hbm, d_hbm, g_hbm,
    out_ref, dq_ref, dk_ref, dv_ref, dd_ref,
    order_ref, doc_ref, q_ref, k_ref, v_ref, d_ref, g_ref, in_sem, decay,
    sx, rx, sy, ry, f_own, f_in, b_own, b_in, doc_prev, doc_next,
    x_send, x_recv, y_send, y_recv, f_send, f_recv, b_send, b_recv, doc_send, doc_recv,
):
    me = lax.axis_index("dp")
    pos = lax.axis_index("ctx")
    rows = q_hbm.shape[1]
    pairs = q_hbm.shape[2] // KW
    blocks = rows // BLK
    per = blocks // n_dp
    part = per * BLK
    has_prev = pos > 0
    has_next = pos < n_ctx - 1

    barrier = pltpu.get_barrier_semaphore()
    for r in range(1, n_dp):
        peer = lax.rem(me + r, n_dp)
        pl.semaphore_signal(barrier, inc=1, device_id={"dp": peer}, device_id_type=MESH)

    @pl.when(has_prev)
    def _():
        pl.semaphore_signal(barrier, inc=1, device_id={"ctx": pos - 1}, device_id_type=MESH)

    @pl.when(has_next)
    def _():
        pl.semaphore_signal(barrier, inc=1, device_id={"ctx": pos + 1}, device_id_type=MESH)

    fetches = [
        pltpu.make_async_copy(src, dst, in_sem.at[i])
        for i, (src, dst) in enumerate((
            (order_hbm, order_ref), (q_hbm, q_ref), (k_hbm, k_ref), (d_hbm, d_ref),
            (v_hbm, v_ref), (doc_hbm, doc_ref), (g_hbm, g_ref),
        ))
    ]
    for fetch in fetches:
        fetch.start()

    def my_rows(index):
        return pl.ds(pl.multiple_of(index * part, part), part)

    def lanes(h, width):
        return pl.ds(pl.multiple_of(h * width, width), width)

    for fetch in fetches[:5]:
        fetch.wait()

    @pl.when(jnp.logical_not(has_prev))
    def _():
        doc_prev[...] = jnp.full_like(doc_prev, -1)
        f_in[...] = jnp.zeros_like(f_in)

    @pl.when(jnp.logical_not(has_next))
    def _():
        doc_next[...] = jnp.full_like(doc_next, -1)
        b_in[...] = jnp.zeros_like(b_in)

    peers = n_dp - 1 + has_prev.astype(jnp.int32) + has_next.astype(jnp.int32)
    pl.semaphore_wait(barrier, peers)

    def exchange(src, dst, send, recv, h, r):
        peer = lax.rem(me + r, n_dp)
        return pltpu.make_async_remote_copy(
            src_ref=src.at[h, my_rows(peer), :],
            dst_ref=dst.at[h, my_rows(me), :],
            send_sem=send.at[h, r],
            recv_sem=recv.at[h, r],
            device_id={"dp": peer},
            device_id_type=MESH,
        )

    def arrival(src, dst, send, recv, h, r):
        source = lax.rem(me + n_dp - r, n_dp)
        return pltpu.make_async_remote_copy(
            src_ref=src.at[h, my_rows(source), :],
            dst_ref=dst.at[h, my_rows(source), :],
            send_sem=send.at[h, r],
            recv_sem=recv.at[h, r],
            device_id={"dp": source},
            device_id_type=MESH,
        )

    def neighbour(src, dst, send, recv, step):
        return pltpu.make_async_remote_copy(
            src_ref=src, dst_ref=dst, send_sem=send, recv_sem=recv,
            device_id={"ctx": pos + step}, device_id_type=MESH,
        )

    def doc_up():
        return neighbour(doc_ref, doc_prev, doc_send.at[0], doc_recv.at[0], 1)

    def doc_down():
        return neighbour(doc_ref, doc_next, doc_send.at[1], doc_recv.at[1], -1)

    def chain_up(h):
        return neighbour(f_own.at[h], f_in.at[h], f_send.at[h], f_recv.at[h], 1)

    def chain_down(h):
        return neighbour(b_own.at[h], b_in.at[h], b_send.at[h], b_recv.at[h], -1)

    order = [order_ref[me, 0, j] for j in range(blocks)]

    def piece(j):
        return slice(j * BLK, (j + 1) * BLK)

    def stage(h, carry):
        for src, width, at in ((q_ref, KW, 0), (k_ref, KW, KW), (d_ref, KW, 2 * KW), (v_ref, VW, 3 * KW)):
            parts = [src[0, piece(j), lanes(h, width)] for j in range(blocks)]
            for dest in range(blocks):
                chosen = parts[0]
                for j in range(1, blocks):
                    chosen = lax.select(order[j] == dest, parts[j], chosen)
                sx[h, piece(dest), at : at + width] = chosen
        rx[h, my_rows(me), :] = sx[h, my_rows(me), :]
        for r in range(1, n_dp):
            exchange(sx, rx, x_send, x_recv, h, r).start()
        return carry

    lax.fori_loop(0, pairs, stage, 0)

    for fetch in fetches[5:]:
        fetch.wait()

    @pl.when(has_next)
    def _():
        doc_up().start()

    @pl.when(has_prev)
    def _():
        doc_down().start()

    @pl.when(has_prev)
    def _():
        doc_up().wait_recv()

    @pl.when(has_next)
    def _():
        doc_down().wait_recv()

    doc_row = jnp.broadcast_to(doc_ref[...].astype(F32), (rows, rows))
    doc_col = doc_row.T
    first_row = doc_col[0:1, :]
    last_row = doc_col[rows - 1 : rows, :]
    prev_last = jnp.broadcast_to(doc_prev[:, rows - 1 : rows].astype(F32), (1, rows))
    next_first = jnp.broadcast_to(doc_next[:, 0:1].astype(F32), (1, rows))
    use_state = (prev_last == first_row).astype(F32)
    use_carry = (next_first == last_row).astype(F32)
    single = (first_row == last_row).astype(F32)
    pass_state = single * use_state
    pass_carry = single * use_carry
    in_first = (doc_col == first_row).astype(F32)
    in_last = (doc_col == last_row).astype(F32)
    head_w = in_first * use_state
    tail_w = in_last * use_carry
    row_id = lax.broadcasted_iota(jnp.int32, (rows, rows), 0)
    lane_id = lax.broadcasted_iota(jnp.int32, (rows, rows), 1)
    same = (doc_row == doc_col) & (row_id >= lane_id)
    later = ((doc_row == doc_col) & (row_id <= lane_id)).astype(BF16)
    lower = (row_id >= lane_id).astype(BF16)
    in_a = lax.broadcasted_iota(jnp.int32, (rows, KW), 1) < DK
    factor = DK ** (-0.5)

    def load(h):
        q = rx[h, :, 0:KW]
        k = rx[h, :, KW : 2 * KW]
        d = rx[h, :, 2 * KW : 3 * KW]
        v = rx[h, :, 3 * KW : W]
        g = g_ref[0, :, lanes(h, VW)]
        cum = dot(lower, d, NN)
        total = cum[rows - 1 : rows, :]
        growth = jnp.exp(cum)
        shrink = jnp.exp(-cum)
        to_end = jnp.exp(total - cum)
        q_f = q.astype(F32)
        k_f = k.astype(F32)
        return q_f, k_f, v, g, d, growth, shrink, to_end

    def fold(wide):
        return jnp.concatenate([wide[0:DK, 0:DV], wide[DK:KW, DV:VW]], axis=0)

    def spread(tall):
        nil = jnp.zeros((DK, DV), tall.dtype)
        top = jnp.concatenate([tall[0:DK], nil], axis=1)
        low = jnp.concatenate([nil, tall[DK:KW]], axis=1)
        return jnp.concatenate([top, low], axis=0)

    def local(h):
        for r in range(1, n_dp):
            arrival(sx, rx, x_send, x_recv, h, r).wait_recv()
        q_f, k_f, v, g, d, growth, shrink, to_end = load(h)
        f_own[h] = fold(dot(split(k_f * to_end * in_last), v, TN))
        b_own[h] = factor * fold(dot(split(q_f * growth * in_first), g, TN))
        decay[h] = jnp.exp(dot(d, jnp.ones((rows, DV), BF16), TN))

    def finish(h):
        q_f, k_f, v, g, d, growth, shrink, to_end = load(h)
        q_t = q_f * growth
        k_t = k_f * shrink
        k_e = k_f * to_end * tail_w
        zero = jnp.zeros_like(q_t)
        q_2 = split(jnp.concatenate([jnp.where(in_a, q_t, zero), jnp.where(in_a, zero, q_t)], axis=0))
        k_s = split(k_t)
        k_2 = split(jnp.concatenate([jnp.where(in_a, k_t, zero), jnp.where(in_a, zero, k_t)], axis=0))
        same_2 = jnp.concatenate([same, same], axis=0)
        score_2 = split(jnp.where(same_2, dot(q_2, k_s, NT), 0.0))
        v_a, v_b = v[:, 0:DV], v[:, DV:VW]
        g_a, g_b = g[:, 0:DV], g[:, DV:VW]
        score_a = both(lambda x: x[0:rows], score_2)
        score_b = both(lambda x: x[rows : 2 * rows], score_2)
        state = both(spread, split(f_in[h]))
        carry = both(spread, split(b_in[h]))
        near = jnp.concatenate([dot(score_a, v_a, NN), dot(score_b, v_b, NN)], axis=1)
        far = dot(split(q_t * head_w), state, NN)
        out_ref[0, :, lanes(h, VW)] = (factor * (near + far)).astype(BF16)
        gs_a = jnp.where(same, dot(g_a, v_a, NT), 0.0)
        gs_b = jnp.where(same, dot(g_b, v_b, NT), 0.0)
        dq_near = dot(split(jnp.concatenate([gs_a, gs_b], axis=1)), k_2, NN)
        dq = factor * growth * (dq_near + dot(g, state, NT) * head_w)
        dk_near = dot(split(jnp.concatenate([gs_a, gs_b], axis=0)), q_2, TN)
        dk = factor * shrink * dk_near + to_end * dot(v, carry, NT) * tail_w
        dv_near = jnp.concatenate([dot(score_a, g_a, TN), dot(score_b, g_b, TN)], axis=1)
        dv = factor * dv_near + dot(split(k_e), carry, NN)
        log_grad = q_f * dq - k_f * dk
        sums = dot(jnp.ones((8, DV), BF16), split(f_own[h] * b_in[h]), NT)
        dd = dot(later, split(log_grad), NN) + sums[0:1] * tail_w
        sy[h, :, 0:KW] = dq.astype(BF16)
        sy[h, :, KW : 2 * KW] = dk.astype(BF16)
        sy[h, :, 2 * KW : 3 * KW] = dd.astype(BF16)
        sy[h, :, 3 * KW : W] = dv.astype(BF16)
        ry[h, my_rows(me), :] = sy[h, my_rows(me), :]
        for r in range(1, n_dp):
            exchange(sy, ry, y_send, y_recv, h, r).start()

    below = n_ctx - 1 - pos
    last_of = jnp.maximum(pos, below)

    def step(t, carry):
        up = t - 1 - pos
        down = t - 1 - below
        ready = t - 1 - last_of

        @pl.when((up >= 0) & (up < pairs))
        def _():
            @pl.when(has_prev)
            def _():
                chain_up(up).wait_recv()

            f_own[up] = f_own[up] + pass_state * decay[up] * f_in[up]

            @pl.when(has_next)
            def _():
                chain_up(up).start()

        @pl.when((down >= 0) & (down < pairs))
        def _():
            @pl.when(has_next)
            def _():
                chain_down(down).wait_recv()

            b_own[down] = b_own[down] + pass_carry * decay[down] * b_in[down]

            @pl.when(has_prev)
            def _():
                chain_down(down).start()

        @pl.when(t < pairs)
        def _():
            local(t)

        @pl.when((ready >= 0) & (ready < pairs))
        def _():
            finish(ready)

        return carry

    lax.fori_loop(0, n_ctx + pairs, step, 0)

    def wait_back(h, carry):
        for r in range(1, n_dp):
            arrival(sy, ry, y_send, y_recv, h, r).wait_recv()
        return carry

    lax.fori_loop(0, pairs, wait_back, 0)

    def unpack(h, carry):
        for dst, width, at in ((dq_ref, KW, 0), (dk_ref, KW, KW), (dd_ref, KW, 2 * KW), (dv_ref, VW, 3 * KW)):
            parts = [ry[h, piece(j), at : at + width] for j in range(blocks)]
            for j in range(blocks):
                chosen = parts[0]
                for place in range(1, blocks):
                    chosen = lax.select(order[j] == place, parts[place], chosen)
                dst[0, piece(j), lanes(h, width)] = chosen
        return carry

    lax.fori_loop(0, pairs, unpack, 0)

    def drain(h, carry):
        for r in range(1, n_dp):
            exchange(sx, rx, x_send, x_recv, h, r).wait_send()
            exchange(sy, ry, y_send, y_recv, h, r).wait_send()

        @pl.when(has_next)
        def _():
            chain_up(h).wait_send()

        @pl.when(has_prev)
        def _():
            chain_down(h).wait_send()

        return carry

    lax.fori_loop(0, pairs, drain, 0)

    @pl.when(has_next)
    def _():
        doc_up().wait_send()

    @pl.when(has_prev)
    def _():
        doc_down().wait_send()


def body(n_dp, n_ctx, query_rows, key_rows, value_rows, log_decay, out_grad, doc_ids, block_order):
    rows, hk = query_rows.shape[1:]
    hv = value_rows.shape[2]
    pairs = hk // KW
    vmem = pl.BlockSpec(memory_space=pltpu.VMEM)
    keys = jax.ShapeDtypeStruct((1, rows, hk), BF16)
    values = jax.ShapeDtypeStruct((1, rows, hv), BF16)
    dma = pltpu.SemaphoreType.DMA
    out, dq, dk, dv, dd = pl.pallas_call(
        functools.partial(kernel, n_dp, n_ctx),
        out_shape=(values, keys, keys, values, keys),
        in_specs=[pl.BlockSpec(memory_space=pltpu.HBM)] * 7,
        out_specs=(vmem,) * 5,
        scratch_shapes=[
            pltpu.SMEM(block_order.shape, jnp.int32),
            pltpu.VMEM((1, rows), jnp.int32),
            pltpu.VMEM((1, rows, hk), BF16),
            pltpu.VMEM((1, rows, hk), BF16),
            pltpu.VMEM((1, rows, hv), BF16),
            pltpu.VMEM((1, rows, hk), BF16),
            pltpu.VMEM((1, rows, hv), BF16),
            dma((7,)),
            pltpu.VMEM((pairs, KW, DV), F32),
            pltpu.VMEM((pairs, rows, W), BF16),
            pltpu.VMEM((pairs, rows, W), BF16),
            pltpu.VMEM((pairs, rows, W), BF16),
            pltpu.VMEM((pairs, rows, W), BF16),
            pltpu.VMEM((pairs, KW, DV), F32),
            pltpu.VMEM((pairs, KW, DV), F32),
            pltpu.VMEM((pairs, KW, DV), F32),
            pltpu.VMEM((pairs, KW, DV), F32),
            pltpu.VMEM((1, rows), jnp.int32),
            pltpu.VMEM((1, rows), jnp.int32),
            dma((pairs, n_dp)), dma((pairs, n_dp)), dma((pairs, n_dp)), dma((pairs, n_dp)),
            dma((pairs,)), dma((pairs,)), dma((pairs,)), dma((pairs,)),
            dma((2,)), dma((2,)),
        ],
        compiler_params=pltpu.CompilerParams(
            collective_id=0, has_side_effects=True, vmem_limit_bytes=40 * 1024 * 1024
        ),
    )(block_order, doc_ids, query_rows, key_rows, value_rows, log_decay, out_grad)
    return out, dq, dk, dv, dd


def solution(mesh):
    placed = P("dp", "ctx", None)
    return jax.shard_map(
        functools.partial(body, mesh.shape["dp"], mesh.shape["ctx"]),
        mesh=mesh,
        in_specs=(placed,) * 5 + (P("dp", "ctx"), P(None, "ctx", None)),
        out_specs=(placed,) * 5,
        check_vma=False,
    )
```

```python
import functools

import jax
import jax.numpy as jnp
from jax import lax
from jax.experimental import pallas as pl
from jax.experimental.pallas import tpu as pltpu
from jax.sharding import PartitionSpec as P

DK = 64
DV = 128
BLK = 32
KW = 2 * DK
VW = 2 * DV
W = 3 * KW + VW
MESH = pl.DeviceIdType.MESH
F32 = jnp.float32
BF16 = jnp.bfloat16

NN = (((1,), (0,)), ((), ()))
NT = (((1,), (1,)), ((), ()))
TN = (((0,), (0,)), ((), ()))


def split(x):
    hi = x.astype(BF16)
    return hi, (x - hi.astype(F32)).astype(BF16)


def dot(a, b, dims):
    a = a if isinstance(a, tuple) else (a,)
    b = b if isinstance(b, tuple) else (b,)
    total = None
    for i, left in enumerate(a):
        for j, right in enumerate(b):
            if i + j > 1:
                continue
            term = lax.dot_general(left, right, dims, preferred_element_type=F32)
            total = term if total is None else total + term
    return total


def both(fn, pair):
    return tuple(fn(x) for x in pair)


def kernel(
    n_dp, n_ctx, order_hbm, doc_hbm, q_hbm, k_hbm, v_hbm, d_hbm, g_hbm,
    out_ref, ry,
    order_ref, doc_ref, q_ref, k_ref, v_ref, d_ref, g_ref, in_sem, decay,
    sx, rx, sy, f_own, f_in, b_own, b_in, doc_prev, doc_next,
    x_send, x_recv, y_send, y_recv, f_send, f_recv, b_send, b_recv, doc_send, doc_recv,
):
    me = lax.axis_index("dp")
    pos = lax.axis_index("ctx")
    rows = q_hbm.shape[1]
    pairs = q_hbm.shape[2] // KW
    blocks = rows // BLK
    per = blocks // n_dp
    part = per * BLK
    has_prev = pos > 0
    has_next = pos < n_ctx - 1

    barrier = pltpu.get_barrier_semaphore()
    for r in range(1, n_dp):
        peer = lax.rem(me + r, n_dp)
        pl.semaphore_signal(barrier, inc=1, device_id={"dp": peer}, device_id_type=MESH)

    @pl.when(has_prev)
    def _():
        pl.semaphore_signal(barrier, inc=1, device_id={"ctx": pos - 1}, device_id_type=MESH)

    @pl.when(has_next)
    def _():
        pl.semaphore_signal(barrier, inc=1, device_id={"ctx": pos + 1}, device_id_type=MESH)

    fetches = [
        pltpu.make_async_copy(src, dst, in_sem.at[i])
        for i, (src, dst) in enumerate((
            (order_hbm, order_ref), (q_hbm, q_ref), (k_hbm, k_ref), (d_hbm, d_ref),
            (v_hbm, v_ref), (doc_hbm, doc_ref), (g_hbm, g_ref),
        ))
    ]
    for fetch in fetches:
        fetch.start()

    def my_rows(index):
        return pl.ds(pl.multiple_of(index * part, part), part)

    def lanes(h, width):
        return pl.ds(pl.multiple_of(h * width, width), width)

    for fetch in fetches[:5]:
        fetch.wait()

    @pl.when(jnp.logical_not(has_prev))
    def _():
        doc_prev[...] = jnp.full_like(doc_prev, -1)
        f_in[...] = jnp.zeros_like(f_in)

    @pl.when(jnp.logical_not(has_next))
    def _():
        doc_next[...] = jnp.full_like(doc_next, -1)
        b_in[...] = jnp.zeros_like(b_in)

    peers = n_dp - 1 + has_prev.astype(jnp.int32) + has_next.astype(jnp.int32)
    pl.semaphore_wait(barrier, peers)

    def exchange(src, dst, send, recv, h, r):
        peer = lax.rem(me + r, n_dp)
        return pltpu.make_async_remote_copy(
            src_ref=src.at[h, my_rows(peer), :],
            dst_ref=dst.at[h, my_rows(me), :],
            send_sem=send.at[h, r],
            recv_sem=recv.at[h, r],
            device_id={"dp": peer},
            device_id_type=MESH,
        )

    def arrival(src, dst, send, recv, h, r):
        source = lax.rem(me + n_dp - r, n_dp)
        return pltpu.make_async_remote_copy(
            src_ref=src.at[h, my_rows(source), :],
            dst_ref=dst.at[h, my_rows(source), :],
            send_sem=send.at[h, r],
            recv_sem=recv.at[h, r],
            device_id={"dp": source},
            device_id_type=MESH,
        )

    def neighbour(src, dst, send, recv, step):
        return pltpu.make_async_remote_copy(
            src_ref=src, dst_ref=dst, send_sem=send, recv_sem=recv,
            device_id={"ctx": pos + step}, device_id_type=MESH,
        )

    def doc_up():
        return neighbour(doc_ref, doc_prev, doc_send.at[0], doc_recv.at[0], 1)

    def doc_down():
        return neighbour(doc_ref, doc_next, doc_send.at[1], doc_recv.at[1], -1)

    def chain_up(h):
        return neighbour(f_own.at[h], f_in.at[h], f_send.at[h], f_recv.at[h], 1)

    def chain_down(h):
        return neighbour(b_own.at[h], b_in.at[h], b_send.at[h], b_recv.at[h], -1)

    order = [order_ref[me, 0, j] for j in range(blocks)]

    def piece(j):
        return slice(j * BLK, (j + 1) * BLK)

    def stage(h, carry):
        for src, width, at in ((q_ref, KW, 0), (k_ref, KW, KW), (d_ref, KW, 2 * KW), (v_ref, VW, 3 * KW)):
            parts = [src[0, piece(j), lanes(h, width)] for j in range(blocks)]
            for dest in range(blocks):
                chosen = parts[0]
                for j in range(1, blocks):
                    chosen = lax.select(order[j] == dest, parts[j], chosen)
                sx[h, piece(dest), at : at + width] = chosen
        rx[h, my_rows(me), :] = sx[h, my_rows(me), :]
        for r in range(1, n_dp):
            exchange(sx, rx, x_send, x_recv, h, r).start()
        return carry

    lax.fori_loop(0, pairs, stage, 0)

    for fetch in fetches[5:]:
        fetch.wait()

    @pl.when(has_next)
    def _():
        doc_up().start()

    @pl.when(has_prev)
    def _():
        doc_down().start()

    @pl.when(has_prev)
    def _():
        doc_up().wait_recv()

    @pl.when(has_next)
    def _():
        doc_down().wait_recv()

    doc_row = jnp.broadcast_to(doc_ref[...].astype(F32), (rows, rows))
    doc_col = doc_row.T
    first_row = doc_col[0:1, :]
    last_row = doc_col[rows - 1 : rows, :]
    prev_last = jnp.broadcast_to(doc_prev[:, rows - 1 : rows].astype(F32), (1, rows))
    next_first = jnp.broadcast_to(doc_next[:, 0:1].astype(F32), (1, rows))
    use_state = (prev_last == first_row).astype(F32)
    use_carry = (next_first == last_row).astype(F32)
    single = (first_row == last_row).astype(F32)
    pass_state = single * use_state
    pass_carry = single * use_carry
    in_first = (doc_col == first_row).astype(F32)
    in_last = (doc_col == last_row).astype(F32)
    head_w = in_first * use_state
    tail_w = in_last * use_carry
    row_id = lax.broadcasted_iota(jnp.int32, (rows, rows), 0)
    lane_id = lax.broadcasted_iota(jnp.int32, (rows, rows), 1)
    same = (doc_row == doc_col) & (row_id >= lane_id)
    later = ((doc_row == doc_col) & (row_id <= lane_id)).astype(BF16)
    lower = (row_id >= lane_id).astype(BF16)
    in_a = lax.broadcasted_iota(jnp.int32, (rows, KW), 1) < DK
    factor = DK ** (-0.5)

    def load(h):
        q = rx[h, :, 0:KW]
        k = rx[h, :, KW : 2 * KW]
        d = rx[h, :, 2 * KW : 3 * KW]
        v = rx[h, :, 3 * KW : W]
        g = g_ref[0, :, lanes(h, VW)]
        cum = dot(lower, d, NN)
        total = cum[rows - 1 : rows, :]
        growth = jnp.exp(cum)
        shrink = jnp.exp(-cum)
        to_end = jnp.exp(total - cum)
        q_f = q.astype(F32)
        k_f = k.astype(F32)
        return q_f, k_f, v, g, d, growth, shrink, to_end

    def fold(wide):
        return jnp.concatenate([wide[0:DK, 0:DV], wide[DK:KW, DV:VW]], axis=0)

    def spread(tall):
        nil = jnp.zeros((DK, DV), tall.dtype)
        top = jnp.concatenate([tall[0:DK], nil], axis=1)
        low = jnp.concatenate([nil, tall[DK:KW]], axis=1)
        return jnp.concatenate([top, low], axis=0)

    def local(h):
        for r in range(1, n_dp):
            arrival(sx, rx, x_send, x_recv, h, r).wait_recv()
        q_f, k_f, v, g, d, growth, shrink, to_end = load(h)
        f_own[h] = fold(dot(split(k_f * to_end * in_last), v, TN))
        b_own[h] = factor * fold(dot(split(q_f * growth * in_first), g, TN))
        decay[h] = jnp.exp(dot(d, jnp.ones((rows, DV), BF16), TN))

    def finish(h):
        q_f, k_f, v, g, d, growth, shrink, to_end = load(h)
        q_t = q_f * growth
        k_t = k_f * shrink
        k_e = k_f * to_end * tail_w
        zero = jnp.zeros_like(q_t)
        q_2 = split(jnp.concatenate([jnp.where(in_a, q_t, zero), jnp.where(in_a, zero, q_t)], axis=0))
        k_s = split(k_t)
        k_2 = split(jnp.concatenate([jnp.where(in_a, k_t, zero), jnp.where(in_a, zero, k_t)], axis=0))
        same_2 = jnp.concatenate([same, same], axis=0)
        score_2 = split(jnp.where(same_2, dot(q_2, k_s, NT), 0.0))
        v_a, v_b = v[:, 0:DV], v[:, DV:VW]
        g_a, g_b = g[:, 0:DV], g[:, DV:VW]
        score_a = both(lambda x: x[0:rows], score_2)
        score_b = both(lambda x: x[rows : 2 * rows], score_2)
        state = both(spread, split(f_in[h]))
        carry = both(spread, split(b_in[h]))
        near = jnp.concatenate([dot(score_a, v_a, NN), dot(score_b, v_b, NN)], axis=1)
        far = dot(split(q_t * head_w), state, NN)
        out_ref[0, :, lanes(h, VW)] = (factor * (near + far)).astype(BF16)
        gs_a = jnp.where(same, dot(g_a, v_a, NT), 0.0)
        gs_b = jnp.where(same, dot(g_b, v_b, NT), 0.0)
        dq_near = dot(split(jnp.concatenate([gs_a, gs_b], axis=1)), k_2, NN)
        dq = factor * growth * (dq_near + dot(g, state, NT) * head_w)
        dk_near = dot(split(jnp.concatenate([gs_a, gs_b], axis=0)), q_2, TN)
        dk = factor * shrink * dk_near + to_end * dot(v, carry, NT) * tail_w
        dv_near = jnp.concatenate([dot(score_a, g_a, TN), dot(score_b, g_b, TN)], axis=1)
        dv = factor * dv_near + dot(split(k_e), carry, NN)
        log_grad = q_f * dq - k_f * dk
        sums = dot(jnp.ones((8, DV), BF16), split(f_own[h] * b_in[h]), NT)
        dd = dot(later, split(log_grad), NN) + sums[0:1] * tail_w
        sy[h, :, 0:KW] = dq.astype(BF16)
        sy[h, :, KW : 2 * KW] = dk.astype(BF16)
        sy[h, :, 2 * KW : 3 * KW] = dd.astype(BF16)
        sy[h, :, 3 * KW : W] = dv.astype(BF16)
        ry[h, my_rows(me), :] = sy[h, my_rows(me), :]
        for r in range(1, n_dp):
            exchange(sy, ry, y_send, y_recv, h, r).start()

    below = n_ctx - 1 - pos
    last_of = jnp.maximum(pos, below)

    def step(t, carry):
        up = t - 1 - pos
        down = t - 1 - below
        ready = t - 1 - last_of

        @pl.when((up >= 0) & (up < pairs))
        def _():
            @pl.when(has_prev)
            def _():
                chain_up(up).wait_recv()

            f_own[up] = f_own[up] + pass_state * decay[up] * f_in[up]

            @pl.when(has_next)
            def _():
                chain_up(up).start()

        @pl.when((down >= 0) & (down < pairs))
        def _():
            @pl.when(has_next)
            def _():
                chain_down(down).wait_recv()

            b_own[down] = b_own[down] + pass_carry * decay[down] * b_in[down]

            @pl.when(has_prev)
            def _():
                chain_down(down).start()

        @pl.when(t < pairs)
        def _():
            local(t)

        @pl.when((ready >= 0) & (ready < pairs))
        def _():
            finish(ready)

        return carry

    lax.fori_loop(0, n_ctx + pairs, step, 0)

    def wait_back(h, carry):
        for r in range(1, n_dp):
            arrival(sy, ry, y_send, y_recv, h, r).wait_recv()
        return carry

    lax.fori_loop(0, pairs, wait_back, 0)

    def drain(h, carry):
        for r in range(1, n_dp):
            exchange(sx, rx, x_send, x_recv, h, r).wait_send()
            exchange(sy, ry, y_send, y_recv, h, r).wait_send()

        @pl.when(has_next)
        def _():
            chain_up(h).wait_send()

        @pl.when(has_prev)
        def _():
            chain_down(h).wait_send()

        return carry

    lax.fori_loop(0, pairs, drain, 0)

    @pl.when(has_next)
    def _():
        doc_up().wait_send()

    @pl.when(has_prev)
    def _():
        doc_down().wait_send()


def unpack(pairs, order_ref, ry, rows_ref, out_ref, dq_ref, dk_ref, dv_ref, dd_ref):
    out_ref[...] = rows_ref[...]
    for h in range(pairs):
        key, value = slice(h * KW, (h + 1) * KW), slice(h * VW, (h + 1) * VW)
        dq_ref[0, :, key] = ry[h, :, 0:KW]
        dk_ref[0, :, key] = ry[h, :, KW : 2 * KW]
        dd_ref[0, :, key] = ry[h, :, 2 * KW : 3 * KW]
        dv_ref[0, :, value] = ry[h, :, 3 * KW : W]


def body(n_dp, n_ctx, query_rows, key_rows, value_rows, log_decay, out_grad, doc_ids, block_order):
    rows, hk = query_rows.shape[1:]
    hv = value_rows.shape[2]
    pairs = hk // KW
    vmem = pl.BlockSpec(memory_space=pltpu.VMEM)
    keys = jax.ShapeDtypeStruct((1, rows, hk), BF16)
    values = jax.ShapeDtypeStruct((1, rows, hv), BF16)
    dma = pltpu.SemaphoreType.DMA
    rows_out, back = pl.pallas_call(
        functools.partial(kernel, n_dp, n_ctx),
        out_shape=(values, jax.ShapeDtypeStruct((pairs, rows, W), BF16)),
        in_specs=[pl.BlockSpec(memory_space=pltpu.HBM)] * 7,
        out_specs=(vmem,) * 2,
        scratch_shapes=[
            pltpu.SMEM(block_order.shape, jnp.int32),
            pltpu.VMEM((1, rows), jnp.int32),
            pltpu.VMEM((1, rows, hk), BF16),
            pltpu.VMEM((1, rows, hk), BF16),
            pltpu.VMEM((1, rows, hv), BF16),
            pltpu.VMEM((1, rows, hk), BF16),
            pltpu.VMEM((1, rows, hv), BF16),
            dma((7,)),
            pltpu.VMEM((pairs, KW, DV), F32),
            pltpu.VMEM((pairs, rows, W), BF16),
            pltpu.VMEM((pairs, rows, W), BF16),
            pltpu.VMEM((pairs, rows, W), BF16),
            pltpu.VMEM((pairs, KW, DV), F32),
            pltpu.VMEM((pairs, KW, DV), F32),
            pltpu.VMEM((pairs, KW, DV), F32),
            pltpu.VMEM((pairs, KW, DV), F32),
            pltpu.VMEM((1, rows), jnp.int32),
            pltpu.VMEM((1, rows), jnp.int32),
            dma((pairs, n_dp)), dma((pairs, n_dp)), dma((pairs, n_dp)), dma((pairs, n_dp)),
            dma((pairs,)), dma((pairs,)), dma((pairs,)), dma((pairs,)),
            dma((2,)), dma((2,)),
        ],
        compiler_params=pltpu.CompilerParams(
            collective_id=0, has_side_effects=True, vmem_limit_bytes=56 * 1024 * 1024
        ),
    )(block_order, doc_ids, query_rows, key_rows, value_rows, log_decay, out_grad)
    key_block = pl.BlockSpec((1, BLK, hk), lambda j, order: (0, j, 0))
    value_block = pl.BlockSpec((1, BLK, hv), lambda j, order: (0, j, 0))
    return pl.pallas_call(
        functools.partial(unpack, pairs),
        out_shape=(values, keys, keys, values, keys),
        grid_spec=pltpu.PrefetchScalarGridSpec(
            num_scalar_prefetch=1,
            grid=(rows // BLK,),
            in_specs=[
                pl.BlockSpec((pairs, BLK, W), lambda j, order: (0, order[lax.axis_index("dp"), 0, j], 0)),
                value_block,
            ],
            out_specs=(value_block, key_block, key_block, value_block, key_block),
        ),
    )(block_order, back, rows_out)


def solution(mesh):
    placed = P("dp", "ctx", None)
    return jax.shard_map(
        functools.partial(body, mesh.shape["dp"], mesh.shape["ctx"]),
        mesh=mesh,
        in_specs=(placed,) * 5 + (P("dp", "ctx"), P(None, "ctx", None)),
        out_specs=(placed,) * 5,
        check_vma=False,
    )
```

```python
import functools

import jax
import jax.numpy as jnp
from jax import lax
from jax.experimental import pallas as pl
from jax.experimental.pallas import tpu as pltpu
from jax.sharding import PartitionSpec as P

DK = 64
DV = 128
BLK = 32
KW = 2 * DK
VW = 2 * DV
W = 3 * KW + VW
MESH = pl.DeviceIdType.MESH
F32 = jnp.float32
BF16 = jnp.bfloat16

NN = (((1,), (0,)), ((), ()))
NT = (((1,), (1,)), ((), ()))
TN = (((0,), (0,)), ((), ()))


def split(x):
    hi = x.astype(BF16)
    return hi, (x - hi.astype(F32)).astype(BF16)


def dot(a, b, dims):
    a = a if isinstance(a, tuple) else (a,)
    b = b if isinstance(b, tuple) else (b,)
    total = None
    for i, left in enumerate(a):
        for j, right in enumerate(b):
            if i + j > 1:
                continue
            term = lax.dot_general(left, right, dims, preferred_element_type=F32)
            total = term if total is None else total + term
    return total


def both(fn, pair):
    return tuple(fn(x) for x in pair)


def kernel(
    n_dp, n_ctx, order_hbm, doc_hbm, q_hbm, k_hbm, v_hbm, d_hbm, g_hbm,
    out_ref, ry,
    order_ref, doc_ref, q_ref, k_ref, v_ref, d_ref, g_ref, in_sem, decay, near, dv_near, dq_near, dk_near,
    sx, rx, sy, f_own, f_in, b_own, b_in, doc_prev, doc_next,
    x_send, x_recv, y_send, y_recv, f_send, f_recv, b_send, b_recv, doc_send, doc_recv,
):
    me = lax.axis_index("dp")
    pos = lax.axis_index("ctx")
    rows = q_hbm.shape[1]
    pairs = q_hbm.shape[2] // KW
    blocks = rows // BLK
    per = blocks // n_dp
    part = per * BLK
    has_prev = pos > 0
    has_next = pos < n_ctx - 1

    barrier = pltpu.get_barrier_semaphore()
    for r in range(1, n_dp):
        peer = lax.rem(me + r, n_dp)
        pl.semaphore_signal(barrier, inc=1, device_id={"dp": peer}, device_id_type=MESH)

    @pl.when(has_prev)
    def _():
        pl.semaphore_signal(barrier, inc=1, device_id={"ctx": pos - 1}, device_id_type=MESH)

    @pl.when(has_next)
    def _():
        pl.semaphore_signal(barrier, inc=1, device_id={"ctx": pos + 1}, device_id_type=MESH)

    fetches = [
        pltpu.make_async_copy(src, dst, in_sem.at[i])
        for i, (src, dst) in enumerate((
            (order_hbm, order_ref), (q_hbm, q_ref), (k_hbm, k_ref), (d_hbm, d_ref),
            (v_hbm, v_ref), (doc_hbm, doc_ref), (g_hbm, g_ref),
        ))
    ]
    for fetch in fetches:
        fetch.start()

    def my_rows(index):
        return pl.ds(pl.multiple_of(index * part, part), part)

    def lanes(h, width):
        return pl.ds(pl.multiple_of(h * width, width), width)

    for fetch in fetches[:5]:
        fetch.wait()

    @pl.when(jnp.logical_not(has_prev))
    def _():
        doc_prev[...] = jnp.full_like(doc_prev, -1)
        f_in[...] = jnp.zeros_like(f_in)

    @pl.when(jnp.logical_not(has_next))
    def _():
        doc_next[...] = jnp.full_like(doc_next, -1)
        b_in[...] = jnp.zeros_like(b_in)

    peers = n_dp - 1 + has_prev.astype(jnp.int32) + has_next.astype(jnp.int32)
    pl.semaphore_wait(barrier, peers)

    def exchange(src, dst, send, recv, h, r):
        peer = lax.rem(me + r, n_dp)
        return pltpu.make_async_remote_copy(
            src_ref=src.at[h, my_rows(peer), :],
            dst_ref=dst.at[h, my_rows(me), :],
            send_sem=send.at[h, r],
            recv_sem=recv.at[h, r],
            device_id={"dp": peer},
            device_id_type=MESH,
        )

    def arrival(src, dst, send, recv, h, r):
        source = lax.rem(me + n_dp - r, n_dp)
        return pltpu.make_async_remote_copy(
            src_ref=src.at[h, my_rows(source), :],
            dst_ref=dst.at[h, my_rows(source), :],
            send_sem=send.at[h, r],
            recv_sem=recv.at[h, r],
            device_id={"dp": source},
            device_id_type=MESH,
        )

    def neighbour(src, dst, send, recv, step):
        return pltpu.make_async_remote_copy(
            src_ref=src, dst_ref=dst, send_sem=send, recv_sem=recv,
            device_id={"ctx": pos + step}, device_id_type=MESH,
        )

    def doc_up():
        return neighbour(doc_ref, doc_prev, doc_send.at[0], doc_recv.at[0], 1)

    def doc_down():
        return neighbour(doc_ref, doc_next, doc_send.at[1], doc_recv.at[1], -1)

    def chain_up(h):
        return neighbour(f_own.at[h], f_in.at[h], f_send.at[h], f_recv.at[h], 1)

    def chain_down(h):
        return neighbour(b_own.at[h], b_in.at[h], b_send.at[h], b_recv.at[h], -1)

    order = [order_ref[me, 0, j] for j in range(blocks)]

    def piece(j):
        return slice(j * BLK, (j + 1) * BLK)

    def stage(h, carry):
        for src, width, at in ((q_ref, KW, 0), (k_ref, KW, KW), (d_ref, KW, 2 * KW), (v_ref, VW, 3 * KW)):
            parts = [src[0, piece(j), lanes(h, width)] for j in range(blocks)]
            for dest in range(blocks):
                chosen = parts[0]
                for j in range(1, blocks):
                    chosen = lax.select(order[j] == dest, parts[j], chosen)
                sx[h, piece(dest), at : at + width] = chosen
        rx[h, my_rows(me), :] = sx[h, my_rows(me), :]
        for r in range(1, n_dp):
            exchange(sx, rx, x_send, x_recv, h, r).start()
        return carry

    lax.fori_loop(0, pairs, stage, 0)

    for fetch in fetches[5:]:
        fetch.wait()

    @pl.when(has_next)
    def _():
        doc_up().start()

    @pl.when(has_prev)
    def _():
        doc_down().start()

    @pl.when(has_prev)
    def _():
        doc_up().wait_recv()

    @pl.when(has_next)
    def _():
        doc_down().wait_recv()

    doc_row = jnp.broadcast_to(doc_ref[...].astype(F32), (rows, rows))
    doc_col = doc_row.T
    first_row = doc_col[0:1, :]
    last_row = doc_col[rows - 1 : rows, :]
    prev_last = jnp.broadcast_to(doc_prev[:, rows - 1 : rows].astype(F32), (1, rows))
    next_first = jnp.broadcast_to(doc_next[:, 0:1].astype(F32), (1, rows))
    use_state = (prev_last == first_row).astype(F32)
    use_carry = (next_first == last_row).astype(F32)
    single = (first_row == last_row).astype(F32)
    pass_state = single * use_state
    pass_carry = single * use_carry
    in_first = (doc_col == first_row).astype(F32)
    in_last = (doc_col == last_row).astype(F32)
    head_w = in_first * use_state
    tail_w = in_last * use_carry
    row_id = lax.broadcasted_iota(jnp.int32, (rows, rows), 0)
    lane_id = lax.broadcasted_iota(jnp.int32, (rows, rows), 1)
    same = (doc_row == doc_col) & (row_id >= lane_id)
    later = ((doc_row == doc_col) & (row_id <= lane_id)).astype(BF16)
    lower = (row_id >= lane_id).astype(BF16)
    in_a = lax.broadcasted_iota(jnp.int32, (rows, KW), 1) < DK
    factor = DK ** (-0.5)

    def load(h):
        q = rx[h, :, 0:KW]
        k = rx[h, :, KW : 2 * KW]
        d = rx[h, :, 2 * KW : 3 * KW]
        v = rx[h, :, 3 * KW : W]
        g = g_ref[0, :, lanes(h, VW)]
        cum = dot(lower, d, NN)
        total = cum[rows - 1 : rows, :]
        growth = jnp.exp(cum)
        shrink = jnp.exp(-cum)
        to_end = jnp.exp(total - cum)
        q_f = q.astype(F32)
        k_f = k.astype(F32)
        return q_f, k_f, v, g, d, growth, shrink, to_end

    def fold(wide):
        return jnp.concatenate([wide[0:DK, 0:DV], wide[DK:KW, DV:VW]], axis=0)

    def spread(tall):
        nil = jnp.zeros((DK, DV), tall.dtype)
        top = jnp.concatenate([tall[0:DK], nil], axis=1)
        low = jnp.concatenate([nil, tall[DK:KW]], axis=1)
        return jnp.concatenate([top, low], axis=0)

    def local(h):
        for r in range(1, n_dp):
            arrival(sx, rx, x_send, x_recv, h, r).wait_recv()
        q_f, k_f, v, g, d, growth, shrink, to_end = load(h)
        f_own[h] = fold(dot(split(k_f * to_end * in_last), v, TN))
        b_own[h] = factor * fold(dot(split(q_f * growth * in_first), g, TN))
        decay[h] = jnp.exp(dot(d, jnp.ones((rows, DV), BF16), TN))

    def inside(h):
        q_f, k_f, v, g, d, growth, shrink, to_end = load(h)
        q_t = q_f * growth
        k_t = k_f * shrink
        zero = jnp.zeros_like(q_t)
        q_2 = split(jnp.concatenate([jnp.where(in_a, q_t, zero), jnp.where(in_a, zero, q_t)], axis=0))
        k_s = split(k_t)
        k_2 = split(jnp.concatenate([jnp.where(in_a, k_t, zero), jnp.where(in_a, zero, k_t)], axis=0))
        same_2 = jnp.concatenate([same, same], axis=0)
        score_2 = split(jnp.where(same_2, dot(q_2, k_s, NT), 0.0))
        v_a, v_b = v[:, 0:DV], v[:, DV:VW]
        g_a, g_b = g[:, 0:DV], g[:, DV:VW]
        score_a = both(lambda x: x[0:rows], score_2)
        score_b = both(lambda x: x[rows : 2 * rows], score_2)
        near[h, :, 0:DV] = dot(score_a, v_a, NN)
        near[h, :, DV:VW] = dot(score_b, v_b, NN)
        dv_near[h, :, 0:DV] = dot(score_a, g_a, TN)
        dv_near[h, :, DV:VW] = dot(score_b, g_b, TN)
        gs_a = jnp.where(same, dot(g_a, v_a, NT), 0.0)
        gs_b = jnp.where(same, dot(g_b, v_b, NT), 0.0)
        dq_near[h] = dot(split(jnp.concatenate([gs_a, gs_b], axis=1)), k_2, NN)
        dk_near[h] = factor * shrink * dot(split(jnp.concatenate([gs_a, gs_b], axis=0)), q_2, TN)

    def finish(h):
        q_f, k_f, v, g, d, growth, shrink, to_end = load(h)
        q_t = q_f * growth
        k_e = k_f * to_end * tail_w
        state = both(spread, split(f_in[h]))
        carry = both(spread, split(b_in[h]))
        far = dot(split(q_t * head_w), state, NN)
        out_ref[0, :, lanes(h, VW)] = (factor * (near[h] + far)).astype(BF16)
        dq = factor * growth * (dq_near[h] + dot(g, state, NT) * head_w)
        dk = dk_near[h] + to_end * dot(v, carry, NT) * tail_w
        dv = factor * dv_near[h] + dot(split(k_e), carry, NN)
        log_grad = q_f * dq - k_f * dk
        sums = dot(jnp.ones((8, DV), BF16), split(f_own[h] * b_in[h]), NT)
        dd = dot(later, split(log_grad), NN) + sums[0:1] * tail_w
        sy[h, :, 0:KW] = dq.astype(BF16)
        sy[h, :, KW : 2 * KW] = dk.astype(BF16)
        sy[h, :, 2 * KW : 3 * KW] = dd.astype(BF16)
        sy[h, :, 3 * KW : W] = dv.astype(BF16)
        ry[h, my_rows(me), :] = sy[h, my_rows(me), :]
        for r in range(1, n_dp):
            exchange(sy, ry, y_send, y_recv, h, r).start()

    below = n_ctx - 1 - pos
    last_of = jnp.maximum(pos, below)

    def step(t, carry):
        up = t - 1 - pos
        down = t - 1 - below
        ready = t - 1 - last_of

        @pl.when((up >= 0) & (up < pairs))
        def _():
            @pl.when(has_prev)
            def _():
                chain_up(up).wait_recv()

            f_own[up] = f_own[up] + pass_state * decay[up] * f_in[up]

            @pl.when(has_next)
            def _():
                chain_up(up).start()

        @pl.when((down >= 0) & (down < pairs))
        def _():
            @pl.when(has_next)
            def _():
                chain_down(down).wait_recv()

            b_own[down] = b_own[down] + pass_carry * decay[down] * b_in[down]

            @pl.when(has_prev)
            def _():
                chain_down(down).start()

        @pl.when((t >= 1) & (t <= pairs))
        def _():
            inside(t - 1)

        @pl.when((ready >= 0) & (ready < pairs))
        def _():
            finish(ready)

        @pl.when(t < pairs)
        def _():
            local(t)

        return carry

    lax.fori_loop(0, n_ctx + pairs, step, 0)

    def wait_back(h, carry):
        for r in range(1, n_dp):
            arrival(sy, ry, y_send, y_recv, h, r).wait_recv()
        return carry

    lax.fori_loop(0, pairs, wait_back, 0)

    def drain(h, carry):
        for r in range(1, n_dp):
            exchange(sx, rx, x_send, x_recv, h, r).wait_send()
            exchange(sy, ry, y_send, y_recv, h, r).wait_send()

        @pl.when(has_next)
        def _():
            chain_up(h).wait_send()

        @pl.when(has_prev)
        def _():
            chain_down(h).wait_send()

        return carry

    lax.fori_loop(0, pairs, drain, 0)

    @pl.when(has_next)
    def _():
        doc_up().wait_send()

    @pl.when(has_prev)
    def _():
        doc_down().wait_send()


def unpack(pairs, order_ref, ry, rows_ref, out_ref, dq_ref, dk_ref, dv_ref, dd_ref):
    out_ref[...] = rows_ref[...]
    for h in range(pairs):
        key, value = slice(h * KW, (h + 1) * KW), slice(h * VW, (h + 1) * VW)
        dq_ref[0, :, key] = ry[h, :, 0:KW]
        dk_ref[0, :, key] = ry[h, :, KW : 2 * KW]
        dd_ref[0, :, key] = ry[h, :, 2 * KW : 3 * KW]
        dv_ref[0, :, value] = ry[h, :, 3 * KW : W]


def body(n_dp, n_ctx, query_rows, key_rows, value_rows, log_decay, out_grad, doc_ids, block_order):
    rows, hk = query_rows.shape[1:]
    hv = value_rows.shape[2]
    pairs = hk // KW
    vmem = pl.BlockSpec(memory_space=pltpu.VMEM)
    keys = jax.ShapeDtypeStruct((1, rows, hk), BF16)
    values = jax.ShapeDtypeStruct((1, rows, hv), BF16)
    dma = pltpu.SemaphoreType.DMA
    rows_out, back = pl.pallas_call(
        functools.partial(kernel, n_dp, n_ctx),
        out_shape=(values, jax.ShapeDtypeStruct((pairs, rows, W), BF16)),
        in_specs=[pl.BlockSpec(memory_space=pltpu.HBM)] * 7,
        out_specs=(vmem,) * 2,
        scratch_shapes=[
            pltpu.SMEM(block_order.shape, jnp.int32),
            pltpu.VMEM((1, rows), jnp.int32),
            pltpu.VMEM((1, rows, hk), BF16),
            pltpu.VMEM((1, rows, hk), BF16),
            pltpu.VMEM((1, rows, hv), BF16),
            pltpu.VMEM((1, rows, hk), BF16),
            pltpu.VMEM((1, rows, hv), BF16),
            dma((7,)),
            pltpu.VMEM((pairs, KW, DV), F32),
            pltpu.VMEM((pairs, rows, VW), F32),
            pltpu.VMEM((pairs, rows, VW), F32),
            pltpu.VMEM((pairs, rows, KW), F32),
            pltpu.VMEM((pairs, rows, KW), F32),
            pltpu.VMEM((pairs, rows, W), BF16),
            pltpu.VMEM((pairs, rows, W), BF16),
            pltpu.VMEM((pairs, rows, W), BF16),
            pltpu.VMEM((pairs, KW, DV), F32),
            pltpu.VMEM((pairs, KW, DV), F32),
            pltpu.VMEM((pairs, KW, DV), F32),
            pltpu.VMEM((pairs, KW, DV), F32),
            pltpu.VMEM((1, rows), jnp.int32),
            pltpu.VMEM((1, rows), jnp.int32),
            dma((pairs, n_dp)), dma((pairs, n_dp)), dma((pairs, n_dp)), dma((pairs, n_dp)),
            dma((pairs,)), dma((pairs,)), dma((pairs,)), dma((pairs,)),
            dma((2,)), dma((2,)),
        ],
        compiler_params=pltpu.CompilerParams(
            collective_id=0, has_side_effects=True, vmem_limit_bytes=56 * 1024 * 1024
        ),
    )(block_order, doc_ids, query_rows, key_rows, value_rows, log_decay, out_grad)
    key_block = pl.BlockSpec((1, BLK, hk), lambda j, order: (0, j, 0))
    value_block = pl.BlockSpec((1, BLK, hv), lambda j, order: (0, j, 0))
    return pl.pallas_call(
        functools.partial(unpack, pairs),
        out_shape=(values, keys, keys, values, keys),
        grid_spec=pltpu.PrefetchScalarGridSpec(
            num_scalar_prefetch=1,
            grid=(rows // BLK,),
            in_specs=[
                pl.BlockSpec((pairs, BLK, W), lambda j, order: (0, order[lax.axis_index("dp"), 0, j], 0)),
                value_block,
            ],
            out_specs=(value_block, key_block, key_block, value_block, key_block),
        ),
    )(block_order, back, rows_out)


def solution(mesh):
    placed = P("dp", "ctx", None)
    return jax.shard_map(
        functools.partial(body, mesh.shape["dp"], mesh.shape["ctx"]),
        mesh=mesh,
        in_specs=(placed,) * 5 + (P("dp", "ctx"), P(None, "ctx", None)),
        out_specs=(placed,) * 5,
        check_vma=False,
    )
```

```python
import functools

import jax
import jax.numpy as jnp
from jax import lax
from jax.experimental import pallas as pl
from jax.experimental.pallas import tpu as pltpu
from jax.sharding import PartitionSpec as P

DK = 64
DV = 128
BLK = 32
KW = 2 * DK
VW = 2 * DV
W = 3 * KW + VW
MESH = pl.DeviceIdType.MESH
F32 = jnp.float32
BF16 = jnp.bfloat16

NN = (((1,), (0,)), ((), ()))
NT = (((1,), (1,)), ((), ()))
TN = (((0,), (0,)), ((), ()))


def split(x):
    hi = x.astype(BF16)
    return hi, (x - hi.astype(F32)).astype(BF16)


def dot(a, b, dims):
    a = a if isinstance(a, tuple) else (a,)
    b = b if isinstance(b, tuple) else (b,)
    total = None
    for i, left in enumerate(a):
        for j, right in enumerate(b):
            if i + j > 1:
                continue
            term = lax.dot_general(left, right, dims, preferred_element_type=F32)
            total = term if total is None else total + term
    return total


def both(fn, pair):
    return tuple(fn(x) for x in pair)


def kernel(
    n_dp, n_ctx, order_hbm, doc_hbm, q_hbm, k_hbm, v_hbm, d_hbm, g_hbm,
    out_ref, ry,
    order_ref, doc_ref, q_ref, k_ref, v_ref, d_ref, g_ref, in_sem, decay, near, dv_near, dq_near, dk_near,
    sx, rx, sy, f_own, f_in, b_own, b_in, doc_prev, doc_next,
    x_send, x_recv, y_send, y_recv, f_send, f_recv, b_send, b_recv, doc_send, doc_recv,
):
    me = lax.axis_index("dp")
    pos = lax.axis_index("ctx")
    rows = q_hbm.shape[1]
    pairs = q_hbm.shape[2] // KW
    blocks = rows // BLK
    per = blocks // n_dp
    part = per * BLK
    has_prev = pos > 0
    has_next = pos < n_ctx - 1

    barrier = pltpu.get_barrier_semaphore()
    for r in range(1, n_dp):
        peer = lax.rem(me + r, n_dp)
        pl.semaphore_signal(barrier, inc=1, device_id={"dp": peer}, device_id_type=MESH)

    @pl.when(has_prev)
    def _():
        pl.semaphore_signal(barrier, inc=1, device_id={"ctx": pos - 1}, device_id_type=MESH)

    @pl.when(has_next)
    def _():
        pl.semaphore_signal(barrier, inc=1, device_id={"ctx": pos + 1}, device_id_type=MESH)

    fetches = [
        pltpu.make_async_copy(src, dst, in_sem.at[i])
        for i, (src, dst) in enumerate((
            (order_hbm, order_ref), (q_hbm, q_ref), (k_hbm, k_ref), (d_hbm, d_ref),
            (v_hbm, v_ref), (doc_hbm, doc_ref), (g_hbm, g_ref),
        ))
    ]
    for fetch in fetches:
        fetch.start()

    def my_rows(index):
        return pl.ds(pl.multiple_of(index * part, part), part)

    def lanes(h, width):
        return pl.ds(pl.multiple_of(h * width, width), width)

    for fetch in fetches[:5]:
        fetch.wait()

    @pl.when(jnp.logical_not(has_prev))
    def _():
        doc_prev[...] = jnp.full_like(doc_prev, -1)
        f_in[...] = jnp.zeros_like(f_in)

    @pl.when(jnp.logical_not(has_next))
    def _():
        doc_next[...] = jnp.full_like(doc_next, -1)
        b_in[...] = jnp.zeros_like(b_in)

    peers = n_dp - 1 + has_prev.astype(jnp.int32) + has_next.astype(jnp.int32)
    pl.semaphore_wait(barrier, peers)

    def exchange(src, dst, send, recv, h, r):
        peer = lax.rem(me + r, n_dp)
        return pltpu.make_async_remote_copy(
            src_ref=src.at[h, my_rows(peer), :],
            dst_ref=dst.at[h, my_rows(me), :],
            send_sem=send.at[h, r],
            recv_sem=recv.at[h, r],
            device_id={"dp": peer},
            device_id_type=MESH,
        )

    def arrival(src, dst, send, recv, h, r):
        source = lax.rem(me + n_dp - r, n_dp)
        return pltpu.make_async_remote_copy(
            src_ref=src.at[h, my_rows(source), :],
            dst_ref=dst.at[h, my_rows(source), :],
            send_sem=send.at[h, r],
            recv_sem=recv.at[h, r],
            device_id={"dp": source},
            device_id_type=MESH,
        )

    def neighbour(src, dst, send, recv, step):
        return pltpu.make_async_remote_copy(
            src_ref=src, dst_ref=dst, send_sem=send, recv_sem=recv,
            device_id={"ctx": pos + step}, device_id_type=MESH,
        )

    def doc_up():
        return neighbour(doc_ref, doc_prev, doc_send.at[0], doc_recv.at[0], 1)

    def doc_down():
        return neighbour(doc_ref, doc_next, doc_send.at[1], doc_recv.at[1], -1)

    def chain_up(h):
        return neighbour(f_own.at[h], f_in.at[h], f_send.at[h], f_recv.at[h], 1)

    def chain_down(h):
        return neighbour(b_own.at[h], b_in.at[h], b_send.at[h], b_recv.at[h], -1)

    order = [order_ref[me, 0, j] for j in range(blocks)]

    def piece(j):
        return slice(j * BLK, (j + 1) * BLK)

    def stage(h, carry):
        for src, width, at in ((q_ref, KW, 0), (k_ref, KW, KW), (d_ref, KW, 2 * KW), (v_ref, VW, 3 * KW)):
            parts = [src[0, piece(j), lanes(h, width)] for j in range(blocks)]
            for dest in range(blocks):
                chosen = parts[0]
                for j in range(1, blocks):
                    chosen = lax.select(order[j] == dest, parts[j], chosen)
                sx[h, piece(dest), at : at + width] = chosen
        rx[h, my_rows(me), :] = sx[h, my_rows(me), :]
        for r in range(1, n_dp):
            exchange(sx, rx, x_send, x_recv, h, r).start()
        return carry

    lax.fori_loop(0, pairs, stage, 0)

    for fetch in fetches[5:]:
        fetch.wait()

    @pl.when(has_next)
    def _():
        doc_up().start()

    @pl.when(has_prev)
    def _():
        doc_down().start()

    @pl.when(has_prev)
    def _():
        doc_up().wait_recv()

    @pl.when(has_next)
    def _():
        doc_down().wait_recv()

    doc_row = jnp.broadcast_to(doc_ref[...].astype(F32), (rows, rows))
    doc_col = doc_row.T
    first_row = doc_col[0:1, :]
    last_row = doc_col[rows - 1 : rows, :]
    prev_last = jnp.broadcast_to(doc_prev[:, rows - 1 : rows].astype(F32), (1, rows))
    next_first = jnp.broadcast_to(doc_next[:, 0:1].astype(F32), (1, rows))
    use_state = (prev_last == first_row).astype(F32)
    use_carry = (next_first == last_row).astype(F32)
    single = (first_row == last_row).astype(F32)
    pass_state = single * use_state
    pass_carry = single * use_carry
    in_first = (doc_col == first_row).astype(F32)
    in_last = (doc_col == last_row).astype(F32)
    head_w = in_first * use_state
    tail_w = in_last * use_carry
    row_id = lax.broadcasted_iota(jnp.int32, (rows, rows), 0)
    lane_id = lax.broadcasted_iota(jnp.int32, (rows, rows), 1)
    same = (doc_row == doc_col) & (row_id >= lane_id)
    later = ((doc_row == doc_col) & (row_id <= lane_id)).astype(BF16)
    lower = (row_id >= lane_id).astype(BF16)
    in_a = lax.broadcasted_iota(jnp.int32, (rows, KW), 1) < DK
    factor = DK ** (-0.5)

    def load(h):
        q = rx[h, :, 0:KW]
        k = rx[h, :, KW : 2 * KW]
        d = rx[h, :, 2 * KW : 3 * KW]
        v = rx[h, :, 3 * KW : W]
        g = g_ref[0, :, lanes(h, VW)]
        cum = dot(lower, d, NN)
        total = cum[rows - 1 : rows, :]
        growth = jnp.exp(cum)
        shrink = jnp.exp(-cum)
        to_end = jnp.exp(total - cum)
        q_f = q.astype(F32)
        k_f = k.astype(F32)
        return q_f, k_f, v, g, d, growth, shrink, to_end

    def fold(wide):
        return jnp.concatenate([wide[0:DK, 0:DV], wide[DK:KW, DV:VW]], axis=0)

    def spread(tall):
        nil = jnp.zeros((DK, DV), tall.dtype)
        top = jnp.concatenate([tall[0:DK], nil], axis=1)
        low = jnp.concatenate([nil, tall[DK:KW]], axis=1)
        return jnp.concatenate([top, low], axis=0)

    def local(h):
        for r in range(1, n_dp):
            arrival(sx, rx, x_send, x_recv, h, r).wait_recv()
        q_f, k_f, v, g, d, growth, shrink, to_end = load(h)
        f_own[h] = fold(dot(split(k_f * to_end * in_last), v, TN))
        b_own[h] = factor * fold(dot(split(q_f * growth * in_first), g, TN))
        decay[h] = jnp.exp(dot(d, jnp.ones((rows, DV), BF16), TN))

    def inside(h):
        q_f, k_f, v, g, d, growth, shrink, to_end = load(h)
        q_t = q_f * growth
        k_t = k_f * shrink
        zero = jnp.zeros_like(q_t)
        q_2 = split(jnp.concatenate([jnp.where(in_a, q_t, zero), jnp.where(in_a, zero, q_t)], axis=0))
        k_s = split(k_t)
        k_2 = split(jnp.concatenate([jnp.where(in_a, k_t, zero), jnp.where(in_a, zero, k_t)], axis=0))
        same_2 = jnp.concatenate([same, same], axis=0)
        score_2 = split(jnp.where(same_2, dot(q_2, k_s, NT), 0.0))
        v_a, v_b = v[:, 0:DV], v[:, DV:VW]
        g_a, g_b = g[:, 0:DV], g[:, DV:VW]
        score_a = both(lambda x: x[0:rows], score_2)
        score_b = both(lambda x: x[rows : 2 * rows], score_2)
        near[h, :, 0:DV] = dot(score_a, v_a, NN)
        near[h, :, DV:VW] = dot(score_b, v_b, NN)
        dv_near[h, :, 0:DV] = dot(score_a, g_a, TN)
        dv_near[h, :, DV:VW] = dot(score_b, g_b, TN)
        gs_a = jnp.where(same, dot(g_a, v_a, NT), 0.0)
        gs_b = jnp.where(same, dot(g_b, v_b, NT), 0.0)
        dq_near[h] = dot(split(jnp.concatenate([gs_a, gs_b], axis=1)), k_2, NN)
        dk_near[h] = factor * shrink * dot(split(jnp.concatenate([gs_a, gs_b], axis=0)), q_2, TN)

    def finish(h):
        q_f, k_f, v, g, d, growth, shrink, to_end = load(h)
        q_t = q_f * growth
        k_e = k_f * to_end * tail_w
        state = both(spread, split(f_in[h]))
        carry = both(spread, split(b_in[h]))
        far = dot(split(q_t * head_w), state, NN)
        out_ref[0, :, lanes(h, VW)] = (factor * (near[h] + far)).astype(BF16)
        dq = factor * growth * (dq_near[h] + dot(g, state, NT) * head_w)
        dk = dk_near[h] + to_end * dot(v, carry, NT) * tail_w
        dv = factor * dv_near[h] + dot(split(k_e), carry, NN)
        log_grad = q_f * dq - k_f * dk
        sums = dot(jnp.ones((8, DV), BF16), split(f_own[h] * b_in[h]), NT)
        dd = dot(later, split(log_grad), NN) + sums[0:1] * tail_w
        sy[h, :, 0:KW] = dq.astype(BF16)
        sy[h, :, KW : 2 * KW] = dk.astype(BF16)
        sy[h, :, 2 * KW : 3 * KW] = dd.astype(BF16)
        sy[h, :, 3 * KW : W] = dv.astype(BF16)
        ry[h, my_rows(me), :] = sy[h, my_rows(me), :]
        for r in range(1, n_dp):
            exchange(sy, ry, y_send, y_recv, h, r).start()

    below = n_ctx - 1 - pos
    last_of = jnp.maximum(pos, below)

    def step(t, carry):
        up = t - 1 - pos
        down = t - 1 - below
        ready = t - 1 - last_of

        @pl.when((up >= 0) & (up < pairs))
        def _():
            @pl.when(has_prev)
            def _():
                chain_up(up).wait_recv()

            f_own[up] = f_own[up] + pass_state * decay[up] * f_in[up]

            @pl.when(has_next)
            def _():
                chain_up(up).start()

        @pl.when((down >= 0) & (down < pairs))
        def _():
            @pl.when(has_next)
            def _():
                chain_down(down).wait_recv()

            b_own[down] = b_own[down] + pass_carry * decay[down] * b_in[down]

            @pl.when(has_prev)
            def _():
                chain_down(down).start()

        @pl.when((t >= 1) & (t <= pairs))
        def _():
            inside(t - 1)

        @pl.when((ready >= 0) & (ready < pairs))
        def _():
            finish(ready)

        @pl.when(t < pairs)
        def _():
            local(t)

        return carry

    lax.fori_loop(0, n_ctx + pairs, step, 0)

    def wait_back(h, carry):
        for r in range(1, n_dp):
            arrival(sy, ry, y_send, y_recv, h, r).wait_recv()
        return carry

    lax.fori_loop(0, pairs, wait_back, 0)

    def drain(h, carry):
        for r in range(1, n_dp):
            exchange(sx, rx, x_send, x_recv, h, r).wait_send()
            exchange(sy, ry, y_send, y_recv, h, r).wait_send()

        @pl.when(has_next)
        def _():
            chain_up(h).wait_send()

        @pl.when(has_prev)
        def _():
            chain_down(h).wait_send()

        return carry

    lax.fori_loop(0, pairs, drain, 0)

    @pl.when(has_next)
    def _():
        doc_up().wait_send()

    @pl.when(has_prev)
    def _():
        doc_down().wait_send()


def unpack(pairs, order_ref, ry, rows_ref, out_ref, dq_ref, dk_ref, dv_ref, dd_ref,
           buf, dq_v, dk_v, dv_v, dd_v, in_sem, out_sem, rows_sem):
    me = lax.axis_index("dp")
    blocks = rows_ref.shape[1] // BLK
    across = pltpu.make_async_copy(rows_ref, out_ref, rows_sem)
    fetches = []
    for j in range(blocks):
        here = pl.ds(pl.multiple_of(order_ref[me, 0, j] * BLK, BLK), BLK)
        fetches.append(pltpu.make_async_copy(ry.at[:, here, :], buf.at[j], in_sem.at[j]))
        fetches[j].start()
    across.start()
    stores = []
    for j in range(blocks):
        fetches[j].wait()
        there = slice(j * BLK, (j + 1) * BLK)
        for h in range(pairs):
            key, value = slice(h * KW, (h + 1) * KW), slice(h * VW, (h + 1) * VW)
            dq_v[0, there, key] = buf[j, h, :, 0:KW]
            dk_v[0, there, key] = buf[j, h, :, KW : 2 * KW]
            dd_v[0, there, key] = buf[j, h, :, 2 * KW : 3 * KW]
            dv_v[0, there, value] = buf[j, h, :, 3 * KW : W]
        for i, (src, dst) in enumerate(((dq_v, dq_ref), (dk_v, dk_ref), (dv_v, dv_ref), (dd_v, dd_ref))):
            store = pltpu.make_async_copy(src.at[:, there, :], dst.at[:, there, :], out_sem.at[j, i])
            store.start()
            stores.append(store)
    for store in stores:
        store.wait()
    across.wait()


def body(n_dp, n_ctx, query_rows, key_rows, value_rows, log_decay, out_grad, doc_ids, block_order):
    rows, hk = query_rows.shape[1:]
    hv = value_rows.shape[2]
    pairs = hk // KW
    vmem = pl.BlockSpec(memory_space=pltpu.VMEM)
    keys = jax.ShapeDtypeStruct((1, rows, hk), BF16)
    values = jax.ShapeDtypeStruct((1, rows, hv), BF16)
    dma = pltpu.SemaphoreType.DMA
    rows_out, back = pl.pallas_call(
        functools.partial(kernel, n_dp, n_ctx),
        out_shape=(values, jax.ShapeDtypeStruct((pairs, rows, W), BF16)),
        in_specs=[pl.BlockSpec(memory_space=pltpu.HBM)] * 7,
        out_specs=(vmem,) * 2,
        scratch_shapes=[
            pltpu.SMEM(block_order.shape, jnp.int32),
            pltpu.VMEM((1, rows), jnp.int32),
            pltpu.VMEM((1, rows, hk), BF16),
            pltpu.VMEM((1, rows, hk), BF16),
            pltpu.VMEM((1, rows, hv), BF16),
            pltpu.VMEM((1, rows, hk), BF16),
            pltpu.VMEM((1, rows, hv), BF16),
            dma((7,)),
            pltpu.VMEM((pairs, KW, DV), F32),
            pltpu.VMEM((pairs, rows, VW), F32),
            pltpu.VMEM((pairs, rows, VW), F32),
            pltpu.VMEM((pairs, rows, KW), F32),
            pltpu.VMEM((pairs, rows, KW), F32),
            pltpu.VMEM((pairs, rows, W), BF16),
            pltpu.VMEM((pairs, rows, W), BF16),
            pltpu.VMEM((pairs, rows, W), BF16),
            pltpu.VMEM((pairs, KW, DV), F32),
            pltpu.VMEM((pairs, KW, DV), F32),
            pltpu.VMEM((pairs, KW, DV), F32),
            pltpu.VMEM((pairs, KW, DV), F32),
            pltpu.VMEM((1, rows), jnp.int32),
            pltpu.VMEM((1, rows), jnp.int32),
            dma((pairs, n_dp)), dma((pairs, n_dp)), dma((pairs, n_dp)), dma((pairs, n_dp)),
            dma((pairs,)), dma((pairs,)), dma((pairs,)), dma((pairs,)),
            dma((2,)), dma((2,)),
        ],
        compiler_params=pltpu.CompilerParams(
            collective_id=0, has_side_effects=True, vmem_limit_bytes=56 * 1024 * 1024
        ),
    )(block_order, doc_ids, query_rows, key_rows, value_rows, log_decay, out_grad)
    hbm = pl.BlockSpec(memory_space=pltpu.HBM)
    key_rows_v, value_rows_v = pltpu.VMEM((1, rows, hk), BF16), pltpu.VMEM((1, rows, hv), BF16)
    return pl.pallas_call(
        functools.partial(unpack, pairs),
        out_shape=(values, keys, keys, values, keys),
        in_specs=[pl.BlockSpec(memory_space=pltpu.SMEM), hbm, hbm],
        out_specs=(hbm,) * 5,
        scratch_shapes=[
            pltpu.VMEM((rows // BLK, pairs, BLK, W), BF16),
            key_rows_v, key_rows_v, value_rows_v, key_rows_v,
            dma((rows // BLK,)), dma((rows // BLK, 4)), dma,
        ],
        compiler_params=pltpu.CompilerParams(vmem_limit_bytes=56 * 1024 * 1024),
    )(block_order, back, rows_out)


def solution(mesh):
    placed = P("dp", "ctx", None)
    return jax.shard_map(
        functools.partial(body, mesh.shape["dp"], mesh.shape["ctx"]),
        mesh=mesh,
        in_specs=(placed,) * 5 + (P("dp", "ctx"), P(None, "ctx", None)),
        out_specs=(placed,) * 5,
        check_vma=False,
    )
```

```python
import functools

import jax
import jax.numpy as jnp
from jax import lax
from jax.experimental import pallas as pl
from jax.experimental.pallas import tpu as pltpu
from jax.sharding import PartitionSpec as P

DK = 64
DV = 128
BLK = 32
KW = 2 * DK
VW = 2 * DV
W = 3 * KW + VW
MESH = pl.DeviceIdType.MESH
F32 = jnp.float32
BF16 = jnp.bfloat16

NN = (((1,), (0,)), ((), ()))
NT = (((1,), (1,)), ((), ()))
TN = (((0,), (0,)), ((), ()))


def split(x):
    hi = x.astype(BF16)
    return hi, (x - hi.astype(F32)).astype(BF16)


def dot(a, b, dims):
    a = a if isinstance(a, tuple) else (a,)
    b = b if isinstance(b, tuple) else (b,)
    total = None
    for i, left in enumerate(a):
        for j, right in enumerate(b):
            if i + j > 1:
                continue
            term = lax.dot_general(left, right, dims, preferred_element_type=F32)
            total = term if total is None else total + term
    return total


def both(fn, pair):
    return tuple(fn(x) for x in pair)


def kernel(
    n_dp, n_ctx, order_hbm, doc_hbm, q_hbm, k_hbm, v_hbm, d_hbm, g_hbm,
    out_ref, ry,
    order_ref, doc_ref, q_ref, k_ref, v_ref, d_ref, g_ref, in_sem, decay, near, dv_near, dq_near, dk_near,
    sx, rx, sy, f_own, f_in, b_own, b_in, doc_prev, doc_next,
    x_send, x_recv, y_send, y_recv, f_send, f_recv, b_send, b_recv, doc_send, doc_recv,
):
    me = lax.axis_index("dp")
    pos = lax.axis_index("ctx")
    rows = q_hbm.shape[1]
    pairs = q_hbm.shape[2] // KW
    blocks = rows // BLK
    per = blocks // n_dp
    part = per * BLK
    has_prev = pos > 0
    has_next = pos < n_ctx - 1

    barrier = pltpu.get_barrier_semaphore()
    for r in range(1, n_dp):
        peer = lax.rem(me + r, n_dp)
        pl.semaphore_signal(barrier, inc=1, device_id={"dp": peer}, device_id_type=MESH)

    @pl.when(has_prev)
    def _():
        pl.semaphore_signal(barrier, inc=1, device_id={"ctx": pos - 1}, device_id_type=MESH)

    @pl.when(has_next)
    def _():
        pl.semaphore_signal(barrier, inc=1, device_id={"ctx": pos + 1}, device_id_type=MESH)

    fetches = [
        pltpu.make_async_copy(src, dst, in_sem.at[i])
        for i, (src, dst) in enumerate((
            (order_hbm, order_ref), (q_hbm, q_ref), (k_hbm, k_ref), (d_hbm, d_ref),
            (v_hbm, v_ref), (doc_hbm, doc_ref), (g_hbm, g_ref),
        ))
    ]
    for fetch in fetches:
        fetch.start()

    def my_rows(index):
        return pl.ds(pl.multiple_of(index * part, part), part)

    def lanes(h, width):
        return pl.ds(pl.multiple_of(h * width, width), width)

    for fetch in fetches[:5]:
        fetch.wait()

    @pl.when(jnp.logical_not(has_prev))
    def _():
        doc_prev[...] = jnp.full_like(doc_prev, -1)
        f_in[...] = jnp.zeros_like(f_in)

    @pl.when(jnp.logical_not(has_next))
    def _():
        doc_next[...] = jnp.full_like(doc_next, -1)
        b_in[...] = jnp.zeros_like(b_in)

    peers = n_dp - 1 + has_prev.astype(jnp.int32) + has_next.astype(jnp.int32)
    pl.semaphore_wait(barrier, peers)

    def exchange(src, dst, send, recv, h, r):
        peer = lax.rem(me + r, n_dp)
        return pltpu.make_async_remote_copy(
            src_ref=src.at[h, my_rows(peer), :],
            dst_ref=dst.at[h, my_rows(me), :],
            send_sem=send.at[h, r],
            recv_sem=recv.at[h, r],
            device_id={"dp": peer},
            device_id_type=MESH,
        )

    def arrival(src, dst, send, recv, h, r):
        source = lax.rem(me + n_dp - r, n_dp)
        return pltpu.make_async_remote_copy(
            src_ref=src.at[h, my_rows(source), :],
            dst_ref=dst.at[h, my_rows(source), :],
            send_sem=send.at[h, r],
            recv_sem=recv.at[h, r],
            device_id={"dp": source},
            device_id_type=MESH,
        )

    def neighbour(src, dst, send, recv, step):
        return pltpu.make_async_remote_copy(
            src_ref=src, dst_ref=dst, send_sem=send, recv_sem=recv,
            device_id={"ctx": pos + step}, device_id_type=MESH,
        )

    def doc_up():
        return neighbour(doc_ref, doc_prev, doc_send.at[0], doc_recv.at[0], 1)

    def doc_down():
        return neighbour(doc_ref, doc_next, doc_send.at[1], doc_recv.at[1], -1)

    def chain_up(h):
        return neighbour(f_own.at[h], f_in.at[h], f_send.at[h], f_recv.at[h], 1)

    def chain_down(h):
        return neighbour(b_own.at[h], b_in.at[h], b_send.at[h], b_recv.at[h], -1)

    order = [order_ref[me, 0, j] for j in range(blocks)]

    def piece(j):
        return slice(j * BLK, (j + 1) * BLK)

    def stage(h, carry):
        for src, width, at in ((q_ref, KW, 0), (k_ref, KW, KW), (d_ref, KW, 2 * KW), (v_ref, VW, 3 * KW)):
            parts = [src[0, piece(j), lanes(h, width)] for j in range(blocks)]
            for dest in range(blocks):
                chosen = parts[0]
                for j in range(1, blocks):
                    chosen = lax.select(order[j] == dest, parts[j], chosen)
                sx[h, piece(dest), at : at + width] = chosen
        rx[h, my_rows(me), :] = sx[h, my_rows(me), :]
        for r in range(1, n_dp):
            exchange(sx, rx, x_send, x_recv, h, r).start()
        return carry

    lax.fori_loop(0, pairs, stage, 0)

    for fetch in fetches[5:]:
        fetch.wait()

    @pl.when(has_next)
    def _():
        doc_up().start()

    @pl.when(has_prev)
    def _():
        doc_down().start()

    @pl.when(has_prev)
    def _():
        doc_up().wait_recv()

    @pl.when(has_next)
    def _():
        doc_down().wait_recv()

    doc_row = jnp.broadcast_to(doc_ref[...].astype(F32), (rows, rows))
    doc_col = doc_row.T
    first_row = doc_col[0:1, :]
    last_row = doc_col[rows - 1 : rows, :]
    prev_last = jnp.broadcast_to(doc_prev[:, rows - 1 : rows].astype(F32), (1, rows))
    next_first = jnp.broadcast_to(doc_next[:, 0:1].astype(F32), (1, rows))
    use_state = (prev_last == first_row).astype(F32)
    use_carry = (next_first == last_row).astype(F32)
    single = (first_row == last_row).astype(F32)
    pass_state = single * use_state
    pass_carry = single * use_carry
    in_first = (doc_col == first_row).astype(F32)
    in_last = (doc_col == last_row).astype(F32)
    head_w = in_first * use_state
    tail_w = in_last * use_carry
    row_id = lax.broadcasted_iota(jnp.int32, (rows, rows), 0)
    lane_id = lax.broadcasted_iota(jnp.int32, (rows, rows), 1)
    same = (doc_row == doc_col) & (row_id >= lane_id)
    later = ((doc_row == doc_col) & (row_id <= lane_id)).astype(BF16)
    lower = (row_id >= lane_id).astype(BF16)
    in_a = lax.broadcasted_iota(jnp.int32, (rows, KW), 1) < DK
    factor = DK ** (-0.5)

    def load(h):
        q = rx[h, :, 0:KW]
        k = rx[h, :, KW : 2 * KW]
        d = rx[h, :, 2 * KW : 3 * KW]
        v = rx[h, :, 3 * KW : W]
        g = g_ref[0, :, lanes(h, VW)]
        cum = dot(lower, d, NN)
        total = cum[rows - 1 : rows, :]
        growth = jnp.exp(cum)
        shrink = jnp.exp(-cum)
        to_end = jnp.exp(total - cum)
        q_f = q.astype(F32)
        k_f = k.astype(F32)
        return q_f, k_f, v, g, d, growth, shrink, to_end

    def fold(wide):
        return jnp.concatenate([wide[0:DK, 0:DV], wide[DK:KW, DV:VW]], axis=0)

    def spread(tall):
        nil = jnp.zeros((DK, DV), tall.dtype)
        top = jnp.concatenate([tall[0:DK], nil], axis=1)
        low = jnp.concatenate([nil, tall[DK:KW]], axis=1)
        return jnp.concatenate([top, low], axis=0)

    def local(h):
        for r in range(1, n_dp):
            arrival(sx, rx, x_send, x_recv, h, r).wait_recv()
        q_f, k_f, v, g, d, growth, shrink, to_end = load(h)
        f_own[h] = fold(dot(split(k_f * to_end * in_last), v, TN))
        b_own[h] = factor * fold(dot(split(q_f * growth * in_first), g, TN))
        decay[h] = jnp.exp(dot(d, jnp.ones((rows, DV), BF16), TN))

    def inside(h):
        q_f, k_f, v, g, d, growth, shrink, to_end = load(h)
        q_t = q_f * growth
        k_t = k_f * shrink
        zero = jnp.zeros_like(q_t)
        q_2 = split(jnp.concatenate([jnp.where(in_a, q_t, zero), jnp.where(in_a, zero, q_t)], axis=0))
        k_s = split(k_t)
        k_2 = split(jnp.concatenate([jnp.where(in_a, k_t, zero), jnp.where(in_a, zero, k_t)], axis=0))
        same_2 = jnp.concatenate([same, same], axis=0)
        score_2 = split(jnp.where(same_2, dot(q_2, k_s, NT), 0.0))
        v_a, v_b = v[:, 0:DV], v[:, DV:VW]
        g_a, g_b = g[:, 0:DV], g[:, DV:VW]
        score_a = both(lambda x: x[0:rows], score_2)
        score_b = both(lambda x: x[rows : 2 * rows], score_2)
        near[h, :, 0:DV] = dot(score_a, v_a, NN)
        near[h, :, DV:VW] = dot(score_b, v_b, NN)
        dv_near[h, :, 0:DV] = dot(score_a, g_a, TN)
        dv_near[h, :, DV:VW] = dot(score_b, g_b, TN)
        gs_a = jnp.where(same, dot(g_a, v_a, NT), 0.0)
        gs_b = jnp.where(same, dot(g_b, v_b, NT), 0.0)
        dq_near[h] = dot(split(jnp.concatenate([gs_a, gs_b], axis=1)), k_2, NN)
        dk_near[h] = factor * shrink * dot(split(jnp.concatenate([gs_a, gs_b], axis=0)), q_2, TN)

    def finish(h):
        q_f, k_f, v, g, d, growth, shrink, to_end = load(h)
        q_t = q_f * growth
        k_e = k_f * to_end * tail_w
        state = both(spread, split(f_in[h]))
        carry = both(spread, split(b_in[h]))
        far = dot(split(q_t * head_w), state, NN)
        out_ref[0, :, lanes(h, VW)] = (factor * (near[h] + far)).astype(BF16)
        dq = factor * growth * (dq_near[h] + dot(g, state, NT) * head_w)
        dk = dk_near[h] + to_end * dot(v, carry, NT) * tail_w
        dv = factor * dv_near[h] + dot(split(k_e), carry, NN)
        log_grad = q_f * dq - k_f * dk
        sums = dot(jnp.ones((8, DV), BF16), split(f_own[h] * b_in[h]), NT)
        dd = dot(later, split(log_grad), NN) + sums[0:1] * tail_w
        sy[h, :, 0:KW] = dq.astype(BF16)
        sy[h, :, KW : 2 * KW] = dk.astype(BF16)
        sy[h, :, 2 * KW : 3 * KW] = dd.astype(BF16)
        sy[h, :, 3 * KW : W] = dv.astype(BF16)
        ry[h, my_rows(me), :] = sy[h, my_rows(me), :]
        for r in range(1, n_dp):
            exchange(sy, ry, y_send, y_recv, h, r).start()

    below = n_ctx - 1 - pos
    last_of = jnp.maximum(pos, below)

    def step(t, carry):
        up = t - 1 - pos
        down = t - 1 - below
        ready = t - 1 - last_of

        @pl.when((up >= 0) & (up < pairs))
        def _():
            @pl.when(has_prev)
            def _():
                chain_up(up).wait_recv()

            f_own[up] = f_own[up] + pass_state * decay[up] * f_in[up]

            @pl.when(has_next)
            def _():
                chain_up(up).start()

        @pl.when((down >= 0) & (down < pairs))
        def _():
            @pl.when(has_next)
            def _():
                chain_down(down).wait_recv()

            b_own[down] = b_own[down] + pass_carry * decay[down] * b_in[down]

            @pl.when(has_prev)
            def _():
                chain_down(down).start()

        @pl.when((t >= 1) & (t <= pairs))
        def _():
            inside(t - 1)

        @pl.when((ready >= 0) & (ready < pairs))
        def _():
            finish(ready)

        @pl.when(t < pairs)
        def _():
            local(t)

        return carry

    lax.fori_loop(0, n_ctx + pairs, step, 0)

    def wait_back(h, carry):
        for r in range(1, n_dp):
            arrival(sy, ry, y_send, y_recv, h, r).wait_recv()
        return carry

    lax.fori_loop(0, pairs, wait_back, 0)

    def drain(h, carry):
        for r in range(1, n_dp):
            exchange(sx, rx, x_send, x_recv, h, r).wait_send()
            exchange(sy, ry, y_send, y_recv, h, r).wait_send()

        @pl.when(has_next)
        def _():
            chain_up(h).wait_send()

        @pl.when(has_prev)
        def _():
            chain_down(h).wait_send()

        return carry

    lax.fori_loop(0, pairs, drain, 0)

    @pl.when(has_next)
    def _():
        doc_up().wait_send()

    @pl.when(has_prev)
    def _():
        doc_down().wait_send()


def unpack(pairs, order_ref, ry, rows_ref, out_ref, dq_ref, dk_ref, dv_ref, dd_ref,
           buf, rows_v, dq_v, dk_v, dv_v, dd_v, in_sem, out_sem, rows_sem):
    me = lax.axis_index("dp")
    blocks = rows_ref.shape[1] // BLK
    rows_in = pltpu.make_async_copy(rows_ref, rows_v, rows_sem.at[0])
    rows_in.start()
    rows_out = pltpu.make_async_copy(rows_v, out_ref, rows_sem.at[1])
    fetches = []
    for j in range(blocks):
        here = pl.ds(pl.multiple_of(order_ref[me, 0, j] * BLK, BLK), BLK)
        fetches.append(pltpu.make_async_copy(ry.at[:, here, :], buf.at[j], in_sem.at[j]))
        fetches[j].start()
    rows_in.wait()
    rows_out.start()
    stores = []
    for j in range(blocks):
        fetches[j].wait()
        there = slice(j * BLK, (j + 1) * BLK)
        for h in range(pairs):
            key, value = slice(h * KW, (h + 1) * KW), slice(h * VW, (h + 1) * VW)
            dq_v[0, there, key] = buf[j, h, :, 0:KW]
            dk_v[0, there, key] = buf[j, h, :, KW : 2 * KW]
            dd_v[0, there, key] = buf[j, h, :, 2 * KW : 3 * KW]
            dv_v[0, there, value] = buf[j, h, :, 3 * KW : W]
        for i, (src, dst) in enumerate(((dq_v, dq_ref), (dk_v, dk_ref), (dv_v, dv_ref), (dd_v, dd_ref))):
            store = pltpu.make_async_copy(src.at[:, there, :], dst.at[:, there, :], out_sem.at[j, i])
            store.start()
            stores.append(store)
    for store in stores:
        store.wait()
    rows_out.wait()


def body(n_dp, n_ctx, query_rows, key_rows, value_rows, log_decay, out_grad, doc_ids, block_order):
    rows, hk = query_rows.shape[1:]
    hv = value_rows.shape[2]
    pairs = hk // KW
    vmem = pl.BlockSpec(memory_space=pltpu.VMEM)
    keys = jax.ShapeDtypeStruct((1, rows, hk), BF16)
    values = jax.ShapeDtypeStruct((1, rows, hv), BF16)
    dma = pltpu.SemaphoreType.DMA
    rows_out, back = pl.pallas_call(
        functools.partial(kernel, n_dp, n_ctx),
        out_shape=(values, jax.ShapeDtypeStruct((pairs, rows, W), BF16)),
        in_specs=[pl.BlockSpec(memory_space=pltpu.HBM)] * 7,
        out_specs=(vmem,) * 2,
        scratch_shapes=[
            pltpu.SMEM(block_order.shape, jnp.int32),
            pltpu.VMEM((1, rows), jnp.int32),
            pltpu.VMEM((1, rows, hk), BF16),
            pltpu.VMEM((1, rows, hk), BF16),
            pltpu.VMEM((1, rows, hv), BF16),
            pltpu.VMEM((1, rows, hk), BF16),
            pltpu.VMEM((1, rows, hv), BF16),
            dma((7,)),
            pltpu.VMEM((pairs, KW, DV), F32),
            pltpu.VMEM((pairs, rows, VW), F32),
            pltpu.VMEM((pairs, rows, VW), F32),
            pltpu.VMEM((pairs, rows, KW), F32),
            pltpu.VMEM((pairs, rows, KW), F32),
            pltpu.VMEM((pairs, rows, W), BF16),
            pltpu.VMEM((pairs, rows, W), BF16),
            pltpu.VMEM((pairs, rows, W), BF16),
            pltpu.VMEM((pairs, KW, DV), F32),
            pltpu.VMEM((pairs, KW, DV), F32),
            pltpu.VMEM((pairs, KW, DV), F32),
            pltpu.VMEM((pairs, KW, DV), F32),
            pltpu.VMEM((1, rows), jnp.int32),
            pltpu.VMEM((1, rows), jnp.int32),
            dma((pairs, n_dp)), dma((pairs, n_dp)), dma((pairs, n_dp)), dma((pairs, n_dp)),
            dma((pairs,)), dma((pairs,)), dma((pairs,)), dma((pairs,)),
            dma((2,)), dma((2,)),
        ],
        compiler_params=pltpu.CompilerParams(
            collective_id=0, has_side_effects=True, vmem_limit_bytes=56 * 1024 * 1024
        ),
    )(block_order, doc_ids, query_rows, key_rows, value_rows, log_decay, out_grad)
    hbm = pl.BlockSpec(memory_space=pltpu.HBM)
    key_rows_v, value_rows_v = pltpu.VMEM((1, rows, hk), BF16), pltpu.VMEM((1, rows, hv), BF16)
    return pl.pallas_call(
        functools.partial(unpack, pairs),
        out_shape=(values, keys, keys, values, keys),
        in_specs=[pl.BlockSpec(memory_space=pltpu.SMEM), hbm, hbm],
        out_specs=(hbm,) * 5,
        scratch_shapes=[
            pltpu.VMEM((rows // BLK, pairs, BLK, W), BF16),
            value_rows_v, key_rows_v, key_rows_v, value_rows_v, key_rows_v,
            dma((rows // BLK,)), dma((rows // BLK, 4)), dma((2,)),
        ],
        compiler_params=pltpu.CompilerParams(vmem_limit_bytes=56 * 1024 * 1024),
    )(block_order, back, rows_out)


def solution(mesh):
    placed = P("dp", "ctx", None)
    return jax.shard_map(
        functools.partial(body, mesh.shape["dp"], mesh.shape["ctx"]),
        mesh=mesh,
        in_specs=(placed,) * 5 + (P("dp", "ctx"), P(None, "ctx", None)),
        out_specs=(placed,) * 5,
        check_vma=False,
    )
```
